32 devices in a mesh: row: 4 (over z), col: 4 (over y, core), rep: 2 (over x).
Axes of the slice: x: 2, y: 2, z: 4, core: 2. Of those that a mesh axis runs over, the one named last changes fastest.
Arguments:
- a_blocks: bfloat16 [96, 17, 128, 128], P(('row', 'col'), None, 'rep'), may hold values from -0.1875 to 0.1875
- b_blocks: bfloat16 [96, 17, 128, 128], P(('row', 'col'), None, 'rep'), may hold values from -6 to 6
- a_extent: int32 [96], P(('row', 'col')), may hold values from 1 to 8, as said below
- b_extent: int32 [96], P(('row', 'col')), may hold values from 1 to 8, as said below
Outputs:
- c_blocks: bfloat16 [96, 33, 128, 128], P(('row', 'col', 'rep'))
The draws below stay inside these ranges and needn't reach their ends.
Inputs may be any that keep to these rules, and one draw needn't show every extreme that they name: Blocks of row i whose offset |a - 8| exceeds a_extent[i] are absent. Blocks of row j whose offset |b - 8| exceeds b_extent[j] are absent.
All inputs are finite; a program needn't handle non-finite values.
Results may differ from the reference program's by a relative error of at most 0.0052.
Values may be sent and summed in bfloat16 or wider, within the bound.
No kernel may reach another device: no remote copies, remote signals or barrier semaphores. Data moves between devices by JAX's collectives and lax.ppermute only.
A program may use at most 128 MiB of HBM per device.

```python
import jax
import jax.numpy as jnp
from jax import lax

BS = 128
W = 8
ROWS_DEV = 6
NB = 96
N_REP = 2


def extent_law(key):
    sparse_key, crowded_key, anchor_key = jax.random.split(key, 3)
    sparse = jax.random.randint(sparse_key, (NB,), 1, W // 2 + 1)
    crowded = jax.random.randint(crowded_key, (NB,), W // 2 + 1, W + 1)
    anchor = jax.random.randint(anchor_key, (), 0, NB)
    offset_row = (jnp.arange(NB) - anchor) % NB
    extent = jnp.where(offset_row < NB // 4, crowded, sparse)
    return jnp.where(offset_row == 0, W, extent).astype(jnp.int32)


def draw_a_extent(key, part):
    return extent_law(jax.random.fold_in(key, 11))


def draw_b_extent(key, part):
    return extent_law(jax.random.fold_in(key, 23))


def shard_levels(own_key, dims, pieces, least, top_value):
    loudness, own = 1.0, jax.random.fold_in(own_key, 6)
    for position, blocks in pieces:
        heights = jnp.exp(jax.random.uniform(jax.random.fold_in(own, position), (blocks,), jnp.float32, least / len(pieces), top_value / len(pieces)))
        loudness = loudness * jnp.repeat(heights, dims[position] // blocks).reshape([-1 if axis == position else 1 for axis in range(len(dims))])
    return loudness


def centred(rng, shape, spread, most, cuts=(), kind=jnp.bfloat16):
    array = spread * jax.random.normal(rng, shape, jnp.float32)
    if cuts:
        array = array * shard_levels(rng, shape, cuts, -0.22, 0.18)
    return jnp.clip(array, -most, most).astype(kind)


def setup_inputs(seed: int = 0) -> dict:
    seeds = jax.random.split(jax.random.key(seed), 5)
    return {
        "a_blocks": centred(seeds[0], (NB, 2 * W + 1, BS, BS), (BS * (W + 1)) ** -0.5, 0.1875, ((0, 16), (2, 2))),
        "b_blocks": centred(seeds[1], (NB, 2 * W + 1, BS, BS), 1.0, 6.0, ((0, 16), (2, 2))),
        "a_extent": draw_a_extent(jax.random.fold_in(seeds[4], 71), 0),
        "b_extent": draw_b_extent(jax.random.fold_in(seeds[4], 71), 0),
    }


def band_mask(extent):
    distance = jnp.abs(jnp.arange(2 * W + 1) - W)
    return (distance[None, :] <= extent[:, None]).astype(jnp.bfloat16)


def reference(a_blocks, b_blocks, a_extent, b_extent):
    a_masked = a_blocks * band_mask(a_extent)[:, :, None, None]
    b_masked = b_blocks * band_mask(b_extent)[:, :, None, None]
    b_wrapped = jnp.concatenate([b_masked[NB - W:], b_masked, b_masked[:W]], axis=0)
    inner_depth = BS // N_REP

    def one_group(anchor):
        a_rows = lax.dynamic_slice_in_dim(a_masked, anchor, ROWS_DEV, 0)
        b_rows = lax.dynamic_slice_in_dim(b_wrapped, anchor, ROWS_DEV + 2 * W, 0)
        summed = jnp.zeros((ROWS_DEV, 4 * W + 1, BS, BS), jnp.float32)
        for slice_index in range(N_REP):
            lower = slice_index * inner_depth
            totals = jnp.zeros((ROWS_DEV, 4 * W + 1, BS, BS), jnp.float32)
            for offset in range(2 * W + 1):
                left_part = a_rows[:, offset, lower:lower + inner_depth, :].astype(jnp.float32)
                right_part = b_rows[offset:offset + ROWS_DEV, :, lower:lower + inner_depth, :].astype(jnp.float32)
                product = jnp.einsum("ikm,ibkn->ibmn", left_part, right_part)
                totals = totals.at[:, offset:offset + 2 * W + 1].add(product)
            rounded = lax.optimization_barrier(totals.astype(jnp.bfloat16))
            summed = summed + rounded.astype(jnp.float32)
        return summed.astype(jnp.bfloat16)

    anchors = jnp.arange(NB // ROWS_DEV, dtype=jnp.int32) * ROWS_DEV
    grouped = lax.map(one_group, anchors)
    return grouped.reshape(NB, 4 * W + 1, BS, BS)
```

```python
import functools

import jax
import jax.numpy as jnp
from jax import lax
from jax.experimental import pallas as pl
from jax.experimental.pallas import tpu as pltpu
from jax.sharding import PartitionSpec as P

RING = ("row", "col")
EVERY = ("row", "col", "rep")
CHUNK_ROWS = 2
EXTRA_ROWS = 2


def band_live(extent, band_width):
    half_band = (band_width - 1) // 2
    distance = jnp.abs(jnp.arange(band_width) - half_band)
    return (distance[None, :] <= extent[:, None]).astype(jnp.bfloat16)


def to_chip_peer(x, ring):
    return lax.ppermute(x, RING, [(g, g ^ 1) for g in range(ring)])


def to_outer_neighbour(x, ring):
    return lax.ppermute(x, RING, [(g, (g + 2 * (g % 2) - 1) % ring) for g in range(ring)])


def to_second_neighbour(x, ring):
    pairs = []
    for g in range(ring):
        owner = g + 1 if g % 2 else g - 1
        pairs.append((2 * g, 2 * ((owner + 2) % ring)))
        pairs.append((2 * g + 1, 2 * ((owner - 2) % ring) + 1))
    return lax.ppermute(x, EVERY, pairs)


def over_rep(x):
    return lax.ppermute(x, "rep", [(0, 1), (1, 0)])


def product_kernel(depth, rows_out, plan, has_partial, *refs):
    refs = list(refs)
    left_ref = refs.pop(0)
    source_refs = [refs.pop(0) for _ in range(plan["sources"])]
    partial_ref = refs.pop(0) if has_partial else None
    out_ref, window, result, row_sem, out_sem = refs
    slots = plan["slots"]
    band = plan["band"]
    block = window.shape[-1]
    pairs = window.shape[0] // 2
    rep = lax.axis_index("rep")
    core = lax.rem(lax.axis_index("col"), 2)

    def row_copy(source, position, slot):
        return pltpu.make_async_copy(
            source.at[position], window.at[pl.ds(slot, band), slot], row_sem.at[slot]
        )

    for rep_value in range(2):
        for core_value in range(2):

            @pl.when((rep == rep_value) & (core == core_value))
            def _(rep_value=rep_value, core_value=core_value):
                for slot, (source, position) in enumerate(plan["where"](rep_value, core_value)):
                    row_copy(source_refs[source], position, slot).start()

    blank = jnp.zeros((depth, block), window.dtype)
    for pair in range(pairs):
        if 2 * pair + 1 < slots:
            window[2 * pair, 2 * pair + 1] = blank
        if 0 <= 2 * pair + 1 - band < slots:
            window[2 * pair + 1, 2 * pair + 1 - band] = blank
        if slots % 2 and slots <= 2 * pair + 1:
            window[2 * pair, slots] = blank
            window[2 * pair + 1, slots] = blank

    waited = 0
    for pair in range(pairs):
        first = max(0, 2 * pair + 1 - band)
        last = min(slots + slots % 2, 2 * pair + 2)
        while waited < min(last, slots):
            row_copy(source_refs[0], 0, waited).wait()
            waited += 1
        span = (last - first) * depth
        left = left_ref[:, first * depth : last * depth]
        right = jnp.concatenate(
            [window[2 * pair + side, first:last].reshape(span, block) for side in range(2)], 1
        )
        total = jnp.dot(left, right, preferred_element_type=jnp.float32).astype(jnp.bfloat16)
        if has_partial:
            total = total.astype(jnp.float32) + partial_ref[pair].astype(jnp.float32)
            total = total.astype(jnp.bfloat16)
            for row in range(rows_out):
                for side in range(2):
                    offset = 2 * pair + side - row
                    if 0 <= offset < 2 * band - 1:
                        result[row, offset] = total[
                            row * block : (row + 1) * block, side * block : (side + 1) * block
                        ]
        else:
            result[pair] = total
    copy = pltpu.make_async_copy(result, out_ref, out_sem)
    copy.start()
    copy.wait()


def half_product(left, sources, where, partial, rows_out, band):
    depth, block = sources[0].shape[2:]
    slots = rows_out + band - 1
    columns = slots + band - 1
    pairs = (columns + 1) // 2
    plan = {"sources": len(sources), "where": where, "slots": slots, "band": band}
    has_partial = partial is not None
    if has_partial:
        out_shape = (rows_out, 2 * band - 1, block, block)
    else:
        out_shape = (pairs, rows_out * block, 2 * block)
    in_specs = [pl.BlockSpec(memory_space=pltpu.VMEM)]
    in_specs += [pl.BlockSpec(memory_space=pl.ANY)] * len(sources)
    operands = [left, *sources]
    if has_partial:
        in_specs.append(pl.BlockSpec(memory_space=pltpu.VMEM))
        operands.append(partial)
    window_slots = slots + slots % 2
    flops = 2 * rows_out * block * depth * slots * band * block
    return pl.pallas_call(
        functools.partial(product_kernel, depth, rows_out, plan, has_partial),
        out_shape=jax.ShapeDtypeStruct(out_shape, jnp.bfloat16),
        in_specs=in_specs,
        out_specs=pl.BlockSpec(memory_space=pl.ANY),
        scratch_shapes=[
            pltpu.VMEM((2 * pairs, window_slots, depth, block), jnp.bfloat16),
            pltpu.VMEM(out_shape, jnp.bfloat16),
            pltpu.SemaphoreType.DMA((slots,)),
            pltpu.SemaphoreType.DMA,
        ],
        compiler_params=pltpu.CompilerParams(vmem_limit_bytes=40 * 2**20),
        cost_estimate=pl.CostEstimate(
            flops=flops, bytes_accessed=12 * 2**20, transcendentals=0
        ),
    )(*operands)


def stacked_left(a_rows):
    rows_out, band, depth, block = a_rows.shape
    slots = rows_out + band - 1
    turned = jnp.transpose(a_rows, (0, 3, 1, 2)).reshape(rows_out, block, band * depth)
    total = (slots + slots % 2) * depth
    lines = [
        jnp.pad(turned[i], ((0, 0), (i * depth, total - (i + band) * depth)))
        for i in range(rows_out)
    ]
    return jnp.concatenate(lines, 0)


def local(a_blocks, b_blocks, a_extent, b_extent):
    rows, band, depth, block = a_blocks.shape
    ring = lax.axis_size("row") * lax.axis_size("col")
    rows_out = rows // lax.axis_size("rep")
    rep = lax.axis_index("rep")
    chunks = rows // CHUNK_ROWS

    b_own = b_blocks * band_live(b_extent, band)[:, :, None, None]
    a_own = a_blocks * band_live(a_extent, band)[:, :, None, None]
    a_keep = lax.dynamic_slice_in_dim(a_own, rows_out * rep, rows_out, 0)
    a_send = lax.dynamic_slice_in_dim(a_own, rows_out * (1 - rep), rows_out, 0)

    def start_for(side, index):
        return jnp.where(side == 0, rows - (index + 1) * CHUNK_ROWS, index * CHUNK_ROWS)

    peer = to_chip_peer(b_own, ring)
    outer = to_outer_neighbour(b_own, ring)
    across = [
        over_rep(lax.dynamic_slice_in_dim(b_own, start_for(1 - rep, i), CHUNK_ROWS, 0))
        for i in range(chunks)
    ]
    across_outer = [to_outer_neighbour(x, ring) for x in across]
    across_peer = [to_chip_peer(x, ring) for x in across]
    a_across = over_rep(a_send)
    extra = to_second_neighbour(
        lax.dynamic_slice_in_dim(outer, start_for(rep, 0), EXTRA_ROWS, 0), ring
    )
    across_extra = to_second_neighbour(across_outer[0], ring)

    def window_rows(rep_value, core_value):
        left, right = ("outer", "peer") if core_value == 0 else ("peer", "outer")
        line = [("extra", i) for i in range(EXTRA_ROWS)] if rep_value == 0 else []
        first = 0 if rep_value == 0 else rows_out - EXTRA_ROWS
        line += [(left, i) for i in range(first, rows)]
        line += [("own", i) for i in range(rows)]
        line += [(right, i) for i in range(rows)]
        if rep_value == 0:
            line = line[: rows_out + band - 1]
        else:
            line += [("extra", i) for i in range(EXTRA_ROWS)]
        return line

    def where_near(rep_value, core_value):
        index = {"own": 0, "peer": 1, "outer": 2, "extra": 3}
        return [(index[kind], i) for kind, i in window_rows(rep_value, core_value)]

    def where_far(rep_value, core_value):
        index = {"own": 0, "peer": chunks, "outer": 2 * chunks}
        found = []
        for kind, i in window_rows(rep_value, core_value):
            if kind == "extra":
                found.append((3 * chunks, i))
            else:
                chunk = i // CHUNK_ROWS
                chunk = chunks - 1 - chunk if rep_value == 0 else chunk
                found.append((index[kind] + chunk, i % CHUNK_ROWS))
        return found

    near = half_product(
        stacked_left(a_keep), [b_own, peer, outer, extra], where_near, None, rows_out, band
    )
    far_sources = [*across, *across_peer, *across_outer, across_extra]
    return half_product(stacked_left(a_across), far_sources, where_far, near, rows_out, band)


def solution(mesh):
    return jax.shard_map(
        local,
        mesh=mesh,
        in_specs=(
            P(("row", "col"), None, "rep", None),
            P(("row", "col"), None, "rep", None),
            P(("row", "col")),
            P(("row", "col")),
        ),
        out_specs=P(("row", "col", "rep"), None, None, None),
        check_vma=False,
    )
```

```python
import functools

import jax
import jax.numpy as jnp
from jax import lax
from jax.experimental import pallas as pl
from jax.experimental.pallas import tpu as pltpu
from jax.sharding import PartitionSpec as P

RING = ("row", "col")
EVERY = ("row", "col", "rep")
EXTRA_ROWS = 2
REST = 1


def to_chip_peer(x, ring):
    return lax.ppermute(x, RING, [(g, g ^ 1) for g in range(ring)])


def to_outer_neighbour(x, ring):
    return lax.ppermute(x, RING, [(g, (g + 2 * (g % 2) - 1) % ring) for g in range(ring)])


def to_second_neighbour(x, ring):
    pairs = []
    for g in range(ring):
        owner = g + 1 if g % 2 else g - 1
        pairs.append((2 * g, 2 * ((owner + 2) % ring)))
        pairs.append((2 * g + 1, 2 * ((owner - 2) % ring) + 1))
    return lax.ppermute(x, EVERY, pairs)


def over_rep(x):
    return lax.ppermute(x, "rep", [(0, 1), (1, 0)])


def turn_kernel(rows_out, extent_ref, a_ref, out_ref):
    rows, band, depth, block = a_ref.shape
    half_band = (band - 1) // 2
    squares = out_ref.shape[2] // (2 * depth)
    blank = jnp.zeros((depth, block), a_ref.dtype)
    for row in range(rows):
        shift = (row % rows_out) % 2
        extent = extent_ref[row]

        def piece(offset):
            if not 0 <= offset < band:
                return blank
            return jnp.where(abs(offset - half_band) <= extent, a_ref[row, offset], blank)

        for square in range(squares):
            offset = 2 * square - shift
            both = jnp.concatenate([piece(offset), piece(offset + 1)], 0)
            out_ref[row, :, square * 2 * depth : (square + 1) * 2 * depth] = both.T


def turned_left(a_blocks, a_extent, rows_out):
    rows, band, depth, block = a_blocks.shape
    return pl.pallas_call(
        functools.partial(turn_kernel, rows_out),
        out_shape=jax.ShapeDtypeStruct((rows, block, (band + 1) * depth), a_blocks.dtype),
        in_specs=[
            pl.BlockSpec(memory_space=pltpu.SMEM),
            pl.BlockSpec(memory_space=pltpu.VMEM),
        ],
        out_specs=pl.BlockSpec(memory_space=pltpu.VMEM),
        cost_estimate=pl.CostEstimate(
            flops=0, bytes_accessed=8 * a_blocks.size, transcendentals=0
        ),
    )(a_extent, a_blocks)


def product_kernel(plan, *refs):
    refs = list(refs)
    turned_ref = refs.pop(0)
    source_refs = [refs.pop(0) for _ in range(plan["sources"])]
    has_partial = plan["partial"]
    partial_ref = refs.pop(0) if has_partial else None
    out_ref, left, window, result, left_sem, row_sem, out_sem = refs[:7]
    if has_partial:
        partial, partial_sem = refs[7:]
    slots, band, rows_out, depth = plan["slots"], plan["band"], plan["rows_out"], plan["depth"]
    block = window.shape[-1]
    pairs = window.shape[0] // 2
    rep = lax.axis_index("rep")
    core = lax.rem(lax.axis_index("col"), 2)
    first_row = rows_out * rep if plan["own_left"] else 0
    reach = (band + 1) * depth

    def left_copy(row):
        at = (row - row % 2) * depth
        return pltpu.make_async_copy(
            turned_ref.at[first_row + row],
            left.at[pl.ds(row * block, block), pl.ds(at, reach)],
            left_sem.at[row],
        )

    def row_copy(source, position, slot):
        return pltpu.make_async_copy(
            source.at[position], window.at[pl.ds(slot, band), slot], row_sem.at[slot]
        )

    def partial_copy(pair):
        return pltpu.make_async_copy(
            partial_ref.at[pair], partial.at[pair], partial_sem.at[pair]
        )

    def out_copy(pair):
        if has_partial:
            low = max(0, 2 * pair - rows_out + 1)
            high = min(2 * pair - rows_out + 3, 2 * band - 1)
            return pltpu.make_async_copy(
                result.at[:, pl.ds(low, high - low)],
                out_ref.at[:, pl.ds(low, high - low)],
                out_sem.at[pair],
            )
        return pltpu.make_async_copy(result.at[pair], out_ref.at[pair], out_sem.at[pair])

    for row in range(rows_out):
        left_copy(row).start()
    for rep_value in range(2):
        for core_value in range(2):

            @pl.when((rep == rep_value) & (core == core_value))
            def _(rep_value=rep_value, core_value=core_value):
                for slot, (source, position) in enumerate(plan["where"](rep_value, core_value)):
                    row_copy(source_refs[source], position, slot).start()

    if has_partial:
        for pair in range(pairs):
            partial_copy(pair).start()

    width = left.shape[1]
    for row in range(rows_out):
        at = (row - row % 2) * depth
        if at:
            left[row * block : (row + 1) * block, :at] = jnp.zeros((block, at), left.dtype)
        if at + reach < width:
            rest = width - at - reach
            left[row * block : (row + 1) * block, at + reach :] = jnp.zeros(
                (block, rest), left.dtype
            )
    blank = jnp.zeros((depth, block), window.dtype)
    for pair in range(pairs):
        if 2 * pair + 1 < slots:
            window[2 * pair, 2 * pair + 1] = blank
        if 0 <= 2 * pair + 1 - band < slots:
            window[2 * pair + 1, 2 * pair + 1 - band] = blank
        if slots % 2 and slots <= 2 * pair + 1:
            window[2 * pair, slots] = blank
            window[2 * pair + 1, slots] = blank
    for row in range(rows_out):
        left_copy(row).wait()

    waited = 0
    for pair in range(pairs):
        first = max(0, 2 * pair + 1 - band)
        last = min(slots + slots % 2, 2 * pair + 2)
        while waited < min(last, slots):
            row_copy(source_refs[0], 0, waited).wait()
            waited += 1
        span = (last - first) * depth
        right = jnp.concatenate(
            [window[2 * pair + side, first:last].reshape(span, block) for side in range(2)], 1
        )
        total = jnp.dot(
            left[:, first * depth : last * depth], right, preferred_element_type=jnp.float32
        ).astype(jnp.bfloat16)
        if has_partial:
            partial_copy(pair).wait()
            total = total.astype(jnp.float32) + partial[pair].astype(jnp.float32)
            total = total.astype(jnp.bfloat16)
            for row in range(rows_out):
                for side in range(2):
                    offset = 2 * pair + side - row
                    if 0 <= offset < 2 * band - 1:
                        result[row, offset] = total[
                            row * block : (row + 1) * block, side * block : (side + 1) * block
                        ]
        else:
            result[pair] = total
        if pair >= plan["first_out"]:
            out_copy(pair).start()
    for pair in range(plan["first_out"], pairs):
        out_copy(pair).wait()


def half_product(turned, sources, where, partial, rows_out, own_left):
    band, depth, block = sources[0].shape[1:]
    slots = rows_out + band - 1
    columns = slots + band - 1
    pairs = (columns + 1) // 2
    has_partial = partial is not None
    plan = {
        "sources": len(sources),
        "where": where,
        "slots": slots,
        "band": band,
        "rows_out": rows_out,
        "depth": depth,
        "own_left": own_left,
        "partial": has_partial,
        "first_out": (rows_out - 1) // 2 if has_partial else 0,
    }
    operands = [turned, *sources]
    pair_shape = (pairs, rows_out * block, 2 * block)
    if has_partial:
        out_shape = (rows_out, 2 * band - 1, block, block)
        operands.append(partial)
    else:
        out_shape = pair_shape
    window_slots = slots + slots % 2
    scratch = [
        pltpu.VMEM((rows_out * block, window_slots * depth), jnp.bfloat16),
        pltpu.VMEM((2 * pairs, window_slots, depth, block), jnp.bfloat16),
        pltpu.VMEM(out_shape, jnp.bfloat16),
        pltpu.SemaphoreType.DMA((rows_out,)),
        pltpu.SemaphoreType.DMA((slots,)),
        pltpu.SemaphoreType.DMA((pairs,)),
    ]
    if has_partial:
        scratch += [pltpu.VMEM(pair_shape, jnp.bfloat16), pltpu.SemaphoreType.DMA((pairs,))]
    return pl.pallas_call(
        functools.partial(product_kernel, plan),
        out_shape=jax.ShapeDtypeStruct(out_shape, jnp.bfloat16),
        in_specs=[pl.BlockSpec(memory_space=pl.ANY)] * len(operands),
        out_specs=pl.BlockSpec(memory_space=pl.ANY),
        scratch_shapes=scratch,
        compiler_params=pltpu.CompilerParams(vmem_limit_bytes=40 * 2**20),
        cost_estimate=pl.CostEstimate(flops=0, bytes_accessed=0, transcendentals=0),
    )(*operands)


def local(a_blocks, b_blocks, a_extent, b_extent):
    rows, band, depth, block = a_blocks.shape
    half_band = (band - 1) // 2
    ring = lax.axis_size("row") * lax.axis_size("col")
    rows_out = rows // lax.axis_size("rep")
    rep = lax.axis_index("rep")

    distance = jnp.abs(lax.broadcasted_iota(jnp.int32, b_blocks.shape, 1) - half_band)
    live = distance <= b_extent[:, None, None, None]
    b_own = b_blocks * live.astype(b_blocks.dtype)

    starts = ((rows - EXTRA_ROWS, REST, 0), (0, EXTRA_ROWS, rows - REST))
    sizes = (EXTRA_ROWS, rows - EXTRA_ROWS - REST, REST)

    def rows_for(x, side, index):
        start = jnp.where(side == 0, starts[0][index], starts[1][index])
        return lax.dynamic_slice_in_dim(x, start, sizes[index], 0)

    outer = to_outer_neighbour(b_own, ring)
    across = over_rep(b_own)
    peer = to_chip_peer(b_own, ring)
    turned = turned_left(a_blocks, a_extent, rows_out)
    turned_send = lax.dynamic_slice_in_dim(turned, rows_out * (1 - rep), rows_out, 0)
    turned_across = over_rep(turned_send)
    across = lax.optimization_barrier((across, turned_send))[0]
    across_outer = [to_outer_neighbour(rows_for(across, rep, i), ring) for i in range(2)]
    across_peer = to_chip_peer(across, ring)
    extra = to_second_neighbour(rows_for(outer, rep, 0), ring)
    across_outer.append(over_rep(rows_for(outer, 1 - rep, 2)))
    across_extra = to_second_neighbour(across_outer[0], ring)

    def window_rows(rep_value, core_value):
        left, right = ("outer", "peer") if core_value == 0 else ("peer", "outer")
        line = [("extra", i) for i in range(EXTRA_ROWS)] if rep_value == 0 else []
        first = 0 if rep_value == 0 else rows_out - EXTRA_ROWS
        line += [(left, i) for i in range(first, rows)]
        line += [("own", i) for i in range(rows)]
        line += [(right, i) for i in range(rows)]
        if rep_value == 0:
            line = line[: rows_out + band - 1]
        else:
            line += [("extra", i) for i in range(EXTRA_ROWS)]
        return line

    def where_near(rep_value, core_value):
        index = {"own": 0, "peer": 1, "outer": 2, "extra": 3}
        return [(index[kind], i) for kind, i in window_rows(rep_value, core_value)]

    def where_far(rep_value, core_value):
        found = []
        for kind, i in window_rows(rep_value, core_value):
            if kind == "outer":
                spans = zip(starts[rep_value], sizes)
                piece = [low <= i < low + size for low, size in spans].index(True)
                found.append((2 + piece, i - starts[rep_value][piece]))
            else:
                found.append(({"own": 0, "peer": 1, "extra": 5}[kind], i))
        return found

    near = half_product(
        turned, [b_own, peer, outer, extra], where_near, None, rows_out, True
    )
    far_sources = [across, across_peer, *across_outer, across_extra]
    return half_product(turned_across, far_sources, where_far, near, rows_out, False)


def solution(mesh):
    return jax.shard_map(
        local,
        mesh=mesh,
        in_specs=(
            P(("row", "col"), None, "rep", None),
            P(("row", "col"), None, "rep", None),
            P(("row", "col")),
            P(("row", "col")),
        ),
        out_specs=P(("row", "col", "rep"), None, None, None),
        check_vma=False,
    )
```

```python
import functools

import jax
import jax.numpy as jnp
from jax import lax
from jax.experimental import pallas as pl
from jax.experimental.pallas import tpu as pltpu
from jax.sharding import PartitionSpec as P

RING = ("row", "col")
EVERY = ("row", "col", "rep")
EXTRA_ROWS = 2
REST = 1
VMEM_LIMIT = 24 * 2**20


def to_chip_peer(x, ring):
    return lax.ppermute(x, RING, [(g, g ^ 1) for g in range(ring)])


def to_outer_neighbour(x, ring):
    return lax.ppermute(x, RING, [(g, (g + 2 * (g % 2) - 1) % ring) for g in range(ring)])


def to_second_neighbour(x, ring):
    pairs = []
    for g in range(ring):
        owner = g + 1 if g % 2 else g - 1
        pairs.append((2 * g, 2 * ((owner + 2) % ring)))
        pairs.append((2 * g + 1, 2 * ((owner - 2) % ring) + 1))
    return lax.ppermute(x, EVERY, pairs)


def over_rep(x):
    return lax.ppermute(x, "rep", [(0, 1), (1, 0)])


def turn_kernel(rows_out, extent_ref, a_ref, out_ref):
    rows, band, depth, block = a_ref.shape
    half_band = (band - 1) // 2
    squares = out_ref.shape[2] // (2 * depth)
    blank = jnp.zeros((depth, block), a_ref.dtype)
    for row in range(rows):
        shift = first_slot(row // rows_out, row % rows_out) % 2
        extent = extent_ref[row]

        def piece(offset):
            if not 0 <= offset < band:
                return blank
            return jnp.where(abs(offset - half_band) <= extent, a_ref[row, offset], blank)

        for square in range(squares):
            offset = 2 * square - shift
            both = jnp.concatenate([piece(offset), piece(offset + 1)], 0)
            out_ref[row, :, square * 2 * depth : (square + 1) * 2 * depth] = both.T


def turned_left(a_blocks, a_extent, rows_out):
    rows, band, depth, block = a_blocks.shape
    return pl.pallas_call(
        functools.partial(turn_kernel, rows_out),
        out_shape=jax.ShapeDtypeStruct((rows, block, (band + 1) * depth), a_blocks.dtype),
        in_specs=[
            pl.BlockSpec(memory_space=pltpu.SMEM),
            pl.BlockSpec(memory_space=pltpu.VMEM),
        ],
        out_specs=pl.BlockSpec(memory_space=pltpu.VMEM),
        cost_estimate=pl.CostEstimate(
            flops=0, bytes_accessed=8 * a_blocks.size, transcendentals=0
        ),
    )(a_extent, a_blocks)


def first_slot(rep_value, row):
    return row + rep_value


def product_kernel(plan, *refs):
    refs = list(refs)
    turned_ref = refs.pop(0)
    source_refs = [refs.pop(0) for _ in range(plan["sources"])]
    partial_ref = refs.pop(0) if plan["partial"] else None
    out_ref, left, window, left_sem, row_sem = refs[:5]
    final = plan["final"]
    if final:
        result, out_sem = refs[5:]
    band, rows_out = plan["band"], plan["rows_out"]
    columns, slots, depth, block = window.shape
    pairs = columns // 2
    reach = (band + 1) * depth
    width = slots * depth
    rep = lax.axis_index("rep")
    core = lax.rem(lax.axis_index("col"), 2)
    first_row = rows_out * rep if plan["own_left"] else 0

    def left_copy(row, at):
        return pltpu.make_async_copy(
            turned_ref.at[first_row + row],
            left.at[pl.ds(row * block, block), pl.ds(at, reach)],
            left_sem.at[row],
        )

    def row_copy(source, position, slot, index):
        return pltpu.make_async_copy(
            source.at[position], window.at[pl.ds(slot, band), slot], row_sem.at[index]
        )

    def out_copy(half, row):
        low = half * (band - 1)
        count = band - 1 if half == 0 else band
        return pltpu.make_async_copy(
            result.at[row, pl.ds(first_slot(rep, row) + low, count)],
            out_ref.at[row, pl.ds(low, count)],
            out_sem.at[half, row],
        )

    def place_left(rep_value):
        for row in range(rows_out):
            at = first_slot(rep_value, row) // 2 * 2 * depth
            left_copy(row, at).start()
            lines = slice(row * block, (row + 1) * block)
            if at:
                left[lines, :at] = jnp.zeros((block, at), left.dtype)
            if at + reach < width:
                left[lines, at + reach :] = jnp.zeros((block, width - at - reach), left.dtype)

    def place_rows(listed):
        for index, (slot, source, position) in enumerate(listed):
            row_copy(source_refs[source], position, slot, index).start()
        blank = jnp.zeros((depth, block), window.dtype)
        taken = {slot for slot, _, _ in listed}
        for pair in range(pairs):
            if 2 * pair + 1 in taken:
                window[2 * pair, 2 * pair + 1] = blank
            if 2 * pair + 1 - band in taken:
                window[2 * pair + 1, 2 * pair + 1 - band] = blank

    def multiply(ranges, some_pairs):
        for pair in some_pairs:
            total = None
            for low, high in ranges:
                first, last = max(low, 2 * pair + 1 - band), min(high, 2 * pair + 2)
                if first >= last:
                    continue
                span = (last - first) * depth
                right = jnp.concatenate(
                    [
                        window[2 * pair + side, first:last].reshape(span, block)
                        for side in range(2)
                    ],
                    1,
                )
                term = jnp.dot(
                    left[:, first * depth : last * depth],
                    right,
                    preferred_element_type=jnp.float32,
                )
                total = term if total is None else total + term
            if partial_ref is not None:
                before = partial_ref[pair].astype(jnp.float32)
                total = before if total is None else total + before
            if not final:
                out_ref[pair] = total.astype(out_ref.dtype)
                continue
            total = total.astype(result.dtype)
            for row in range(rows_out):
                for side in range(2):
                    result[row, 2 * pair + side] = total[
                        row * block : (row + 1) * block, side * block : (side + 1) * block
                    ]

    for rep_value in range(2):

        @pl.when(rep == rep_value)
        def _(rep_value=rep_value):
            place_left(rep_value)

        for core_value in range(2):

            @pl.when((rep == rep_value) & (core == core_value))
            def _(rep_value=rep_value, core_value=core_value):
                place_rows(plan["where"](rep_value, core_value))

    for row in range(rows_out):
        left_copy(row, 0).wait()
    for index in range(plan["taken"]):
        row_copy(source_refs[0], 0, 0, index).wait()

    parts = [range(pairs)]
    if final:
        middle = (band - 1 + rows_out) // 2 + 1
        parts = [range(middle), range(middle, pairs)]
    for half, part in enumerate(parts):
        if plan["taken"] == slots:
            multiply([(0, slots)], part)
        else:
            for rep_value in range(2):
                for core_value in range(2):

                    @pl.when((rep == rep_value) & (core == core_value))
                    def _(rep_value=rep_value, core_value=core_value, part=part):
                        taken = sorted(slot for slot, _, _ in plan["where"](rep_value, core_value))
                        lows = [slot for slot in taken if slot - 1 not in taken]
                        highs = [slot + 1 for slot in taken if slot + 1 not in taken]
                        multiply(list(zip(lows, highs)), part)

        if final:
            for row in range(rows_out):
                out_copy(half, row).start()
    if final:
        for half in range(2):
            for row in range(rows_out):
                out_copy(half, row).wait()


def partial_product(turned, sources, where, partial, rows_out, own_left, kind):
    band, depth, block = sources[0].shape[1:]
    slots = rows_out + band
    columns = slots + band - 1
    taken = len(where(0, 0))
    final = kind is None
    plan = {
        "sources": len(sources),
        "where": where,
        "taken": taken,
        "band": band,
        "rows_out": rows_out,
        "own_left": own_left,
        "partial": partial is not None,
        "final": final,
    }
    operands = [turned, *sources]
    in_specs = [pl.BlockSpec(memory_space=pl.ANY)] * len(operands)
    if partial is not None:
        operands.append(partial)
        in_specs.append(pl.BlockSpec(memory_space=pltpu.VMEM))
    scratch = [
        pltpu.VMEM((rows_out * block, slots * depth), jnp.bfloat16),
        pltpu.VMEM((columns, slots, depth, block), jnp.bfloat16),
        pltpu.SemaphoreType.DMA((rows_out,)),
        pltpu.SemaphoreType.DMA((taken,)),
    ]
    if final:
        out_shape = jax.ShapeDtypeStruct((rows_out, 2 * band - 1, block, block), jnp.bfloat16)
        out_spec = pl.BlockSpec(memory_space=pl.ANY)
        scratch += [
            pltpu.VMEM((rows_out, columns, block, block), jnp.bfloat16),
            pltpu.SemaphoreType.DMA((2, rows_out)),
        ]
    else:
        out_shape = pltpu.VMEM((columns // 2, rows_out * block, 2 * block), kind)
        out_spec = pl.BlockSpec(memory_space=pltpu.VMEM)
    return pl.pallas_call(
        functools.partial(product_kernel, plan),
        out_shape=out_shape,
        in_specs=in_specs,
        out_specs=out_spec,
        scratch_shapes=scratch,
        compiler_params=pltpu.CompilerParams(vmem_limit_bytes=VMEM_LIMIT),
        cost_estimate=pl.CostEstimate(flops=0, bytes_accessed=0, transcendentals=0),
    )(*operands)


def local(a_blocks, b_blocks, a_extent, b_extent):
    rows, band, depth, block = a_blocks.shape
    half_band = (band - 1) // 2
    ring = lax.axis_size("row") * lax.axis_size("col")
    rows_out = rows // lax.axis_size("rep")
    rep = lax.axis_index("rep")

    distance = jnp.abs(lax.broadcasted_iota(jnp.int32, b_blocks.shape, 1) - half_band)
    live = distance <= b_extent[:, None, None, None]
    b_own = b_blocks * live.astype(b_blocks.dtype)

    starts = ((rows - EXTRA_ROWS, REST, 0), (0, EXTRA_ROWS, rows - REST))
    sizes = (EXTRA_ROWS, rows - EXTRA_ROWS - REST, REST)

    def rows_for(x, side, index):
        start = jnp.where(side == 0, starts[0][index], starts[1][index])
        return lax.dynamic_slice_in_dim(x, start, sizes[index], 0)

    outer = to_outer_neighbour(b_own, ring)
    across = over_rep(b_own)
    peer = to_chip_peer(b_own, ring)
    turned = turned_left(a_blocks, a_extent, rows_out)
    turned_send = lax.dynamic_slice_in_dim(turned, rows_out * (1 - rep), rows_out, 0)
    turned_across = over_rep(turned_send)
    across = lax.optimization_barrier((across, turned_send))[0]
    across_outer = [to_outer_neighbour(rows_for(across, rep, i), ring) for i in range(2)]
    across_peer = to_chip_peer(across, ring)
    extra = to_second_neighbour(rows_for(outer, rep, 0), ring)
    across_outer.append(over_rep(rows_for(outer, 1 - rep, 2)))
    across_extra = to_second_neighbour(across_outer[0], ring)

    def window_rows(rep_value, core_value):
        sides = ("outer", "peer") if core_value == 0 else ("peer", "outer")
        line = [(kind, i) for kind in (sides[0], "own", sides[1]) for i in range(rows)]
        extra_line = [("extra", i) for i in range(EXTRA_ROWS)]
        return extra_line + line if rep_value == 0 else line + extra_line

    def where_of(index):
        def where(rep_value, core_value):
            found = []
            for slot, (kind, i) in enumerate(window_rows(rep_value, core_value)):
                if kind not in index:
                    continue
                source = index[kind]
                if isinstance(source, tuple):
                    spans = zip(starts[rep_value], sizes)
                    piece = [low <= i < low + size for low, size in spans].index(True)
                    found.append((slot, source[piece], i - starts[rep_value][piece]))
                else:
                    found.append((slot, source, i))
            return found

        return where

    total = partial_product(
        turned,
        [b_own, peer, outer, extra],
        where_of({"own": 0, "peer": 1, "outer": 2, "extra": 3}),
        None,
        rows_out,
        True,
        jnp.bfloat16,
    )
    total = partial_product(
        turned_across,
        [across, across_peer],
        where_of({"own": 0, "peer": 1}),
        total,
        rows_out,
        False,
        jnp.float32,
    )
    return partial_product(
        turned_across,
        [*across_outer, across_extra],
        where_of({"outer": (0, 1, 2), "extra": 3}),
        total,
        rows_out,
        False,
        None,
    )


def solution(mesh):
    return jax.shard_map(
        local,
        mesh=mesh,
        in_specs=(
            P(("row", "col"), None, "rep", None),
            P(("row", "col"), None, "rep", None),
            P(("row", "col")),
            P(("row", "col")),
        ),
        out_specs=P(("row", "col", "rep"), None, None, None),
        check_vma=False,
    )
```

```python
import functools

import jax
import jax.numpy as jnp
from jax import lax
from jax.experimental import pallas as pl
from jax.experimental.pallas import tpu as pltpu
from jax.sharding import PartitionSpec as P

RING = ("row", "col")
EVERY = ("row", "col", "rep")
EXTRA_ROWS = 2
REST = 1
VMEM_LIMIT = 24 * 2**20


def to_chip_peer(x, ring):
    return lax.ppermute(x, RING, [(g, g ^ 1) for g in range(ring)])


def to_outer_neighbour(x, ring):
    return lax.ppermute(x, RING, [(g, (g + 2 * (g % 2) - 1) % ring) for g in range(ring)])


def to_second_neighbour(x, ring):
    pairs = []
    for g in range(ring):
        owner = g + 1 if g % 2 else g - 1
        pairs.append((2 * g, 2 * ((owner + 2) % ring)))
        pairs.append((2 * g + 1, 2 * ((owner - 2) % ring) + 1))
    return lax.ppermute(x, EVERY, pairs)


def over_rep(x):
    return lax.ppermute(x, "rep", [(0, 1), (1, 0)])


def turn_kernel(rows_out, extent_ref, a_ref, keep_ref, send_ref):
    rows, band, depth, block = a_ref.shape
    half_band = (band - 1) // 2
    squares = keep_ref.shape[2] // (2 * depth)
    blank = jnp.zeros((depth, block), a_ref.dtype)
    rep = lax.axis_index("rep")

    def turn(row, into_ref):
        shift = first_slot(row // rows_out, row % rows_out) % 2
        extent = extent_ref[row]

        def piece(offset):
            if not 0 <= offset < band:
                return blank
            return jnp.where(abs(offset - half_band) <= extent, a_ref[row, offset], blank)

        for square in range(squares):
            offset = 2 * square - shift
            both = jnp.concatenate([piece(offset), piece(offset + 1)], 0)
            into_ref[row % rows_out, :, square * 2 * depth : (square + 1) * 2 * depth] = both.T

    for rep_value in range(rows // rows_out):

        @pl.when(rep == rep_value)
        def _(rep_value=rep_value):
            for row in range(rows):
                turn(row, keep_ref if row // rows_out == rep_value else send_ref)


def turned_left(a_blocks, a_extent, rows_out):
    rows, band, depth, block = a_blocks.shape
    shape = jax.ShapeDtypeStruct((rows_out, block, (band + 1) * depth), a_blocks.dtype)
    return pl.pallas_call(
        functools.partial(turn_kernel, rows_out),
        out_shape=(shape, shape),
        in_specs=[
            pl.BlockSpec(memory_space=pltpu.SMEM),
            pl.BlockSpec(memory_space=pltpu.VMEM),
        ],
        out_specs=(pl.BlockSpec(memory_space=pltpu.VMEM),) * 2,
        compiler_params=pltpu.CompilerParams(vmem_limit_bytes=8 * 2**20),
        cost_estimate=pl.CostEstimate(flops=0, bytes_accessed=0, transcendentals=0),
    )(a_extent, a_blocks)


def pick_kernel(spans, x_ref, *refs):
    out_refs, sem = refs[:-1], refs[-1]
    rep = lax.axis_index("rep")

    def copies():
        return [
            pltpu.make_async_copy(
                x_ref.at[pl.ds(jnp.where(rep == 0, low, high), out_ref.shape[0])],
                out_ref,
                sem.at[i],
            )
            for i, ((low, high), out_ref) in enumerate(zip(spans, out_refs))
        ]

    for copy in copies():
        copy.start()
    for copy in copies():
        copy.wait()


def picked(x, spans, sizes):
    shapes = [jax.ShapeDtypeStruct((size, *x.shape[1:]), x.dtype) for size in sizes]
    return pl.pallas_call(
        functools.partial(pick_kernel, spans),
        out_shape=shapes,
        in_specs=[pl.BlockSpec(memory_space=pl.ANY)],
        out_specs=[pl.BlockSpec(memory_space=pl.ANY)] * len(sizes),
        scratch_shapes=[pltpu.SemaphoreType.DMA((len(sizes),))],
        compiler_params=pltpu.CompilerParams(vmem_limit_bytes=2**20),
        cost_estimate=pl.CostEstimate(flops=0, bytes_accessed=0, transcendentals=0),
    )(x)


def first_slot(rep_value, row):
    return row + rep_value


def product_kernel(plan, *refs):
    refs = list(refs)
    extent_ref = refs.pop(0)
    turned_ref = refs.pop(0)
    source_refs = [refs.pop(0) for _ in range(plan["sources"])]
    partial_ref = refs.pop(0) if plan["partial"] else None
    out_ref, left, window, left_sem, row_sem = refs[:5]
    final = plan["final"]
    if final:
        result, out_sem = refs[5:]
    band, rows_out = plan["band"], plan["rows_out"]
    columns, slots, depth, block = window.shape
    pairs = columns // 2
    half_band = (band - 1) // 2
    reach = (band + 1) * depth
    width = slots * depth
    rep = lax.axis_index("rep")
    core = lax.rem(lax.axis_index("col"), 2)

    def left_copy(row, at):
        return pltpu.make_async_copy(
            turned_ref.at[row],
            left.at[pl.ds(row * block, block), pl.ds(at, reach)],
            left_sem.at[row],
        )

    def row_copy(source, position, slot, index):
        return pltpu.make_async_copy(
            source.at[position], window.at[pl.ds(slot, band), slot], row_sem.at[index]
        )

    def out_copy(half, row):
        low = half * (band - 1)
        count = band - 1 if half == 0 else band
        return pltpu.make_async_copy(
            result.at[row, pl.ds(first_slot(rep, row) + low, count)],
            out_ref.at[row, pl.ds(low, count)],
            out_sem.at[half, row],
        )

    def place_left(rep_value):
        for row in range(rows_out):
            at = first_slot(rep_value, row) // 2 * 2 * depth
            left_copy(row, at).start()
            lines = slice(row * block, (row + 1) * block)
            if at:
                left[lines, :at] = jnp.zeros((block, at), left.dtype)
            if at + reach < width:
                left[lines, at + reach :] = jnp.zeros((block, width - at - reach), left.dtype)

    def place_rows(listed):
        for index, (slot, source, position) in enumerate(listed):
            row_copy(source_refs[source], position, slot, index).start()
        blank = jnp.zeros((depth, block), window.dtype)
        taken = {slot for slot, _, _ in listed}
        for pair in range(pairs):
            if 2 * pair + 1 in taken:
                window[2 * pair, 2 * pair + 1] = blank
            if 2 * pair + 1 - band in taken:
                window[2 * pair + 1, 2 * pair + 1 - band] = blank

    def multiply(ranges, some_pairs):
        for pair in some_pairs:
            total = None
            for low, high in ranges:
                first, last = max(low, 2 * pair + 1 - band), min(high, 2 * pair + 2)
                if first >= last:
                    continue
                span = (last - first) * depth
                right = jnp.concatenate(
                    [
                        window[2 * pair + side, first:last].reshape(span, block)
                        for side in range(2)
                    ],
                    1,
                )
                term = jnp.dot(
                    left[:, first * depth : last * depth],
                    right,
                    preferred_element_type=jnp.float32,
                )
                total = term if total is None else total + term
            if partial_ref is not None:
                before = partial_ref[pair].astype(jnp.float32)
                total = before if total is None else total + before
            if not final:
                out_ref[pair] = total.astype(out_ref.dtype)
                continue
            total = total.astype(result.dtype)
            for row in range(rows_out):
                for side in range(2):
                    result[row, 2 * pair + side] = total[
                        row * block : (row + 1) * block, side * block : (side + 1) * block
                    ]

    for rep_value in range(2):

        @pl.when(rep == rep_value)
        def _(rep_value=rep_value):
            place_left(rep_value)

        for core_value in range(2):

            @pl.when((rep == rep_value) & (core == core_value))
            def _(rep_value=rep_value, core_value=core_value):
                place_rows(plan["where"](rep_value, core_value))

    def blank_absent(slot):
        row_count = extent_ref.shape[0]
        rows = 2 * rows_out
        group = lax.axis_index("row") * lax.axis_size("col") + lax.axis_index("col")
        place = group * rows + slot - half_band + rep * (half_band - rows)
        extent = extent_ref[lax.rem(place + row_count, row_count)]
        blank = jnp.zeros((depth, block), window.dtype)

        def clear(offset, carry):
            window[slot + offset, slot] = blank
            window[slot + band - 1 - offset, slot] = blank
            return carry

        lax.fori_loop(0, half_band - extent, clear, 0)

    for row in range(rows_out):
        left_copy(row, 0).wait()
    for index in range(plan["taken"]):
        row_copy(source_refs[0], 0, 0, index).wait()
    if plan["taken"] == slots:
        for slot in range(slots):
            blank_absent(slot)
    else:
        for rep_value in range(2):
            for core_value in range(2):

                @pl.when((rep == rep_value) & (core == core_value))
                def _(rep_value=rep_value, core_value=core_value):
                    for slot, _, _ in plan["where"](rep_value, core_value):
                        blank_absent(slot)

    parts = [range(pairs)]
    if final:
        middle = (band - 1 + rows_out) // 2 + 1
        parts = [range(middle), range(middle, pairs)]
    for half, part in enumerate(parts):
        if plan["taken"] == slots:
            multiply([(0, slots)], part)
        else:
            for rep_value in range(2):
                for core_value in range(2):

                    @pl.when((rep == rep_value) & (core == core_value))
                    def _(rep_value=rep_value, core_value=core_value, part=part):
                        taken = sorted(slot for slot, _, _ in plan["where"](rep_value, core_value))
                        lows = [slot for slot in taken if slot - 1 not in taken]
                        highs = [slot + 1 for slot in taken if slot + 1 not in taken]
                        multiply(list(zip(lows, highs)), part)

        if final:
            for row in range(rows_out):
                out_copy(half, row).start()
    if final:
        for half in range(2):
            for row in range(rows_out):
                out_copy(half, row).wait()


def partial_product(extents, turned, sources, where, partial, rows_out, kind):
    band, depth, block = sources[0].shape[1:]
    slots = rows_out + band
    columns = slots + band - 1
    taken = len(where(0, 0))
    final = kind is None
    plan = {
        "sources": len(sources),
        "where": where,
        "taken": taken,
        "band": band,
        "rows_out": rows_out,
        "partial": partial is not None,
        "final": final,
    }
    operands = [extents, turned, *sources]
    in_specs = [pl.BlockSpec(memory_space=pltpu.SMEM)]
    in_specs += [pl.BlockSpec(memory_space=pl.ANY)] * (1 + len(sources))
    if partial is not None:
        operands.append(partial)
        in_specs.append(pl.BlockSpec(memory_space=pltpu.VMEM))
    scratch = [
        pltpu.VMEM((rows_out * block, slots * depth), jnp.bfloat16),
        pltpu.VMEM((columns, slots, depth, block), jnp.bfloat16),
        pltpu.SemaphoreType.DMA((rows_out,)),
        pltpu.SemaphoreType.DMA((taken,)),
    ]
    if final:
        out_shape = jax.ShapeDtypeStruct((rows_out, 2 * band - 1, block, block), jnp.bfloat16)
        out_spec = pl.BlockSpec(memory_space=pl.ANY)
        scratch += [
            pltpu.VMEM((rows_out, columns, block, block), jnp.bfloat16),
            pltpu.SemaphoreType.DMA((2, rows_out)),
        ]
    else:
        out_shape = pltpu.VMEM((columns // 2, rows_out * block, 2 * block), kind)
        out_spec = pl.BlockSpec(memory_space=pltpu.VMEM)
    return pl.pallas_call(
        functools.partial(product_kernel, plan),
        out_shape=out_shape,
        in_specs=in_specs,
        out_specs=out_spec,
        scratch_shapes=scratch,
        compiler_params=pltpu.CompilerParams(vmem_limit_bytes=VMEM_LIMIT),
        cost_estimate=pl.CostEstimate(flops=0, bytes_accessed=0, transcendentals=0),
    )(*operands)


def local(a_blocks, b_blocks, a_extent, b_extent):
    rows, band, depth, block = a_blocks.shape
    ring = lax.axis_size("row") * lax.axis_size("col")
    rows_out = rows // lax.axis_size("rep")

    starts = ((rows - EXTRA_ROWS, REST, 0), (0, EXTRA_ROWS, rows - REST))
    sizes = (EXTRA_ROWS, rows - EXTRA_ROWS - REST, REST)
    spans = list(zip(*starts))

    outer = to_outer_neighbour(b_blocks, ring)
    across = over_rep(b_blocks)
    peer = to_chip_peer(b_blocks, ring)
    extents = lax.all_gather(b_extent, RING, tiled=True)
    turned, turned_send = turned_left(a_blocks, a_extent, rows_out)
    turned_across = over_rep(turned_send)
    across, extents = lax.optimization_barrier((across, turned_send, extents))[::2]
    across_outer = [
        to_outer_neighbour(x, ring) for x in picked(across, spans[:2], sizes[:2])
    ]
    across_peer = to_chip_peer(across, ring)
    extra, rest = picked(outer, [spans[0], spans[2][::-1]], [sizes[0], sizes[2]])
    extra = to_second_neighbour(extra, ring)
    across_outer.append(over_rep(rest))
    across_extra = to_second_neighbour(across_outer[0], ring)

    def window_rows(rep_value, core_value):
        sides = ("outer", "peer") if core_value == 0 else ("peer", "outer")
        line = [(kind, i) for kind in (sides[0], "own", sides[1]) for i in range(rows)]
        extra_line = [("extra", i) for i in range(EXTRA_ROWS)]
        return extra_line + line if rep_value == 0 else line + extra_line

    def where_of(index):
        def where(rep_value, core_value):
            found = []
            for slot, (kind, i) in enumerate(window_rows(rep_value, core_value)):
                if kind not in index:
                    continue
                source = index[kind]
                if isinstance(source, tuple):
                    spans = zip(starts[rep_value], sizes)
                    piece = [low <= i < low + size for low, size in spans].index(True)
                    found.append((slot, source[piece], i - starts[rep_value][piece]))
                else:
                    found.append((slot, source, i))
            return found

        return where

    total = partial_product(
        extents,
        turned,
        [b_blocks, peer, outer, extra],
        where_of({"own": 0, "peer": 1, "outer": 2, "extra": 3}),
        None,
        rows_out,
        jnp.bfloat16,
    )
    total = partial_product(
        extents,
        turned_across,
        [across, across_peer],
        where_of({"own": 0, "peer": 1}),
        total,
        rows_out,
        jnp.float32,
    )
    return partial_product(
        extents,
        turned_across,
        [*across_outer, across_extra],
        where_of({"outer": (0, 1, 2), "extra": 3}),
        total,
        rows_out,
        None,
    )


def solution(mesh):
    return jax.shard_map(
        local,
        mesh=mesh,
        in_specs=(
            P(("row", "col"), None, "rep", None),
            P(("row", "col"), None, "rep", None),
            P(("row", "col")),
            P(("row", "col")),
        ),
        out_specs=P(("row", "col", "rep"), None, None, None),
        check_vma=False,
    )
```

```python
import functools

import jax
import jax.numpy as jnp
from jax import lax
from jax.experimental import pallas as pl
from jax.experimental.pallas import tpu as pltpu
from jax.sharding import PartitionSpec as P

RING = ("row", "col")
EVERY = ("row", "col", "rep")
EXTRA_ROWS = 2
REST = 1
VMEM_LIMIT = 24 * 2**20


def to_chip_peer(x, ring):
    return lax.ppermute(x, RING, [(g, g ^ 1) for g in range(ring)])


def to_outer_neighbour(x, ring):
    return lax.ppermute(x, RING, [(g, (g + 2 * (g % 2) - 1) % ring) for g in range(ring)])


def to_second_neighbour(x, ring):
    pairs = []
    for g in range(ring):
        owner = g + 1 if g % 2 else g - 1
        pairs.append((2 * g, 2 * ((owner + 2) % ring)))
        pairs.append((2 * g + 1, 2 * ((owner - 2) % ring) + 1))
    return lax.ppermute(x, EVERY, pairs)


def over_rep(x):
    return lax.ppermute(x, "rep", [(0, 1), (1, 0)])


def turn_kernel(rows_out, extent_ref, a_ref, keep_ref, send_ref):
    rows, band, depth, block = a_ref.shape
    half_band = (band - 1) // 2
    squares = keep_ref.shape[2] // (2 * depth)
    blank = jnp.zeros((depth, block), a_ref.dtype)
    rep = lax.axis_index("rep")

    def turn(row, into_ref):
        shift = first_slot(row // rows_out, row % rows_out) % 2
        extent = extent_ref[row]

        def piece(offset):
            if not 0 <= offset < band:
                return blank
            return jnp.where(abs(offset - half_band) <= extent, a_ref[row, offset], blank)

        for square in range(squares):
            offset = 2 * square - shift
            both = jnp.concatenate([piece(offset), piece(offset + 1)], 0)
            into_ref[row % rows_out, :, square * 2 * depth : (square + 1) * 2 * depth] = both.T

    for rep_value in range(rows // rows_out):

        @pl.when(rep == rep_value)
        def _(rep_value=rep_value):
            for row in range(rows):
                turn(row, keep_ref if row // rows_out == rep_value else send_ref)


def turned_left(a_blocks, a_extent, rows_out):
    rows, band, depth, block = a_blocks.shape
    shape = jax.ShapeDtypeStruct((rows_out, block, (band + 1) * depth), a_blocks.dtype)
    return pl.pallas_call(
        functools.partial(turn_kernel, rows_out),
        out_shape=(shape, shape),
        in_specs=[
            pl.BlockSpec(memory_space=pltpu.SMEM),
            pl.BlockSpec(memory_space=pltpu.VMEM),
        ],
        out_specs=(pl.BlockSpec(memory_space=pltpu.VMEM),) * 2,
        compiler_params=pltpu.CompilerParams(vmem_limit_bytes=8 * 2**20),
        cost_estimate=pl.CostEstimate(flops=0, bytes_accessed=0, transcendentals=0),
    )(a_extent, a_blocks)


def clear_absent(ref, at, extent, band):
    half_band = (band - 1) // 2

    def clear(offset, carry):
        for b in (offset, band - 1 - offset):
            ref[at(b)] = jnp.zeros(ref.shape[-2:], ref.dtype)
        return carry

    lax.fori_loop(0, half_band - extent, clear, 0)


def pick_kernel(spans, masks, *refs):
    refs = list(refs)
    extent_ref = refs.pop(0) if masks else None
    x_ref, out_refs, sem = refs[0], refs[1:-1], refs[-1]
    rep = lax.axis_index("rep")
    starts = [jnp.where(rep == 0, low, high) for low, high in spans]

    def copies():
        return [
            pltpu.make_async_copy(x_ref.at[pl.ds(start, out_ref.shape[0])], out_ref, sem.at[i])
            for i, (start, out_ref) in enumerate(zip(starts, out_refs))
        ]

    for copy in copies():
        copy.start()
    for copy in copies():
        copy.wait()
    if masks:
        for start, out_ref in zip(starts, out_refs):
            for row in range(out_ref.shape[0]):
                clear_absent(
                    out_ref, lambda b, row=row: (row, b), extent_ref[start + row], out_ref.shape[1]
                )


def picked(x, spans, sizes, extents=None):
    masks = extents is not None
    shapes = [jax.ShapeDtypeStruct((size, *x.shape[1:]), x.dtype) for size in sizes]
    out_space = pltpu.VMEM if masks else pl.ANY
    in_specs = [pl.BlockSpec(memory_space=pltpu.SMEM)] if masks else []
    return pl.pallas_call(
        functools.partial(pick_kernel, spans, masks),
        out_shape=shapes,
        in_specs=in_specs + [pl.BlockSpec(memory_space=pl.ANY)],
        out_specs=[pl.BlockSpec(memory_space=out_space)] * len(sizes),
        scratch_shapes=[pltpu.SemaphoreType.DMA((len(sizes),))],
        compiler_params=pltpu.CompilerParams(vmem_limit_bytes=(4 if masks else 1) * 2**20),
        cost_estimate=pl.CostEstimate(flops=0, bytes_accessed=0, transcendentals=0),
    )(*([extents] if masks else []), x)


def after(x, *others):
    return lax.optimization_barrier((x, *others))[0]


def first_slot(rep_value, row):
    return row + rep_value


def product_kernel(plan, *refs):
    refs = list(refs)
    extent_ref = refs.pop(0) if plan["masked_source"] is not None else None
    turned_ref = refs.pop(0)
    source_refs = [refs.pop(0) for _ in range(plan["sources"])]
    partial_ref = refs.pop(0) if plan["partial"] else None
    out_ref, left, window, left_sem, row_sem = refs[:5]
    final = plan["final"]
    if final:
        result, out_sem = refs[5:]
    band, rows_out = plan["band"], plan["rows_out"]
    columns, slots, depth, block = window.shape
    pairs = columns // 2
    reach = (band + 1) * depth
    width = slots * depth
    rep = lax.axis_index("rep")
    core = lax.rem(lax.axis_index("col"), 2)

    def left_copy(row, at):
        return pltpu.make_async_copy(
            turned_ref.at[row],
            left.at[pl.ds(row * block, block), pl.ds(at, reach)],
            left_sem.at[row],
        )

    def row_copy(source, position, slot, index):
        return pltpu.make_async_copy(
            source.at[position], window.at[pl.ds(slot, band), slot], row_sem.at[index]
        )

    def out_copy(half, row):
        low = half * (band - 1)
        count = band - 1 if half == 0 else band
        return pltpu.make_async_copy(
            result.at[row, pl.ds(first_slot(rep, row) + low, count)],
            out_ref.at[row, pl.ds(low, count)],
            out_sem.at[half, row],
        )

    def place_left(rep_value):
        for row in range(rows_out):
            at = first_slot(rep_value, row) // 2 * 2 * depth
            left_copy(row, at).start()
            lines = slice(row * block, (row + 1) * block)
            if at:
                left[lines, :at] = jnp.zeros((block, at), left.dtype)
            if at + reach < width:
                left[lines, at + reach :] = jnp.zeros((block, width - at - reach), left.dtype)

    def place_rows(listed):
        for index, (slot, source, position) in enumerate(listed):
            row_copy(source_refs[source], position, slot, index).start()
        blank = jnp.zeros((depth, block), window.dtype)
        taken = {slot for slot, _, _ in listed}
        for pair in range(pairs):
            if 2 * pair + 1 in taken:
                window[2 * pair, 2 * pair + 1] = blank
            if 2 * pair + 1 - band in taken:
                window[2 * pair + 1, 2 * pair + 1 - band] = blank

    def multiply(ranges, some_pairs):
        for pair in some_pairs:
            total = None
            for low, high in ranges:
                first, last = max(low, 2 * pair + 1 - band), min(high, 2 * pair + 2)
                if first >= last:
                    continue
                span = (last - first) * depth
                right = jnp.concatenate(
                    [
                        window[2 * pair + side, first:last].reshape(span, block)
                        for side in range(2)
                    ],
                    1,
                )
                term = jnp.dot(
                    left[:, first * depth : last * depth],
                    right,
                    preferred_element_type=jnp.float32,
                )
                total = term if total is None else total + term
            if partial_ref is not None:
                before = partial_ref[pair].astype(jnp.float32)
                total = before if total is None else total + before
            if not final:
                out_ref[pair] = total.astype(out_ref.dtype)
                continue
            total = total.astype(result.dtype)
            for row in range(rows_out):
                for side in range(2):
                    result[row, 2 * pair + side] = total[
                        row * block : (row + 1) * block, side * block : (side + 1) * block
                    ]

    for rep_value in range(2):

        @pl.when(rep == rep_value)
        def _(rep_value=rep_value):
            place_left(rep_value)

        for core_value in range(2):

            @pl.when((rep == rep_value) & (core == core_value))
            def _(rep_value=rep_value, core_value=core_value):
                place_rows(plan["where"](rep_value, core_value))

    for row in range(rows_out):
        left_copy(row, 0).wait()
    for index in range(plan["taken"]):
        row_copy(source_refs[0], 0, 0, index).wait()
    if extent_ref is not None:
        for rep_value in range(2):
            for core_value in range(2):

                @pl.when((rep == rep_value) & (core == core_value))
                def _(rep_value=rep_value, core_value=core_value):
                    for slot, source, position in plan["where"](rep_value, core_value):
                        if source == plan["masked_source"]:
                            clear_absent(
                                window,
                                lambda b, slot=slot: (slot + b, slot),
                                extent_ref[position],
                                band,
                            )

    parts = [range(pairs)]
    if final:
        middle = (band - 1 + rows_out) // 2 + 1
        parts = [range(middle), range(middle, pairs)]
    for half, part in enumerate(parts):
        if plan["taken"] == slots:
            multiply([(0, slots)], part)
        else:
            for rep_value in range(2):
                for core_value in range(2):

                    @pl.when((rep == rep_value) & (core == core_value))
                    def _(rep_value=rep_value, core_value=core_value, part=part):
                        taken = sorted(slot for slot, _, _ in plan["where"](rep_value, core_value))
                        lows = [slot for slot in taken if slot - 1 not in taken]
                        highs = [slot + 1 for slot in taken if slot + 1 not in taken]
                        multiply(list(zip(lows, highs)), part)

        if final:
            for row in range(rows_out):
                out_copy(half, row).start()
    if final:
        for half in range(2):
            for row in range(rows_out):
                out_copy(half, row).wait()


def partial_product(turned, sources, where, partial, rows_out, kind, masked=None):
    band, depth, block = sources[0].shape[1:]
    slots = rows_out + band
    columns = slots + band - 1
    taken = len(where(0, 0))
    final = kind is None
    plan = {
        "sources": len(sources),
        "where": where,
        "taken": taken,
        "band": band,
        "rows_out": rows_out,
        "partial": partial is not None,
        "final": final,
        "masked_source": None if masked is None else masked[0],
    }
    operands = [turned, *sources]
    in_specs = [pl.BlockSpec(memory_space=pl.ANY)] * len(operands)
    if masked is not None:
        operands.insert(0, masked[1])
        in_specs.insert(0, pl.BlockSpec(memory_space=pltpu.SMEM))
    if partial is not None:
        operands.append(partial)
        in_specs.append(pl.BlockSpec(memory_space=pltpu.VMEM))
    scratch = [
        pltpu.VMEM((rows_out * block, slots * depth), jnp.bfloat16),
        pltpu.VMEM((columns, slots, depth, block), jnp.bfloat16),
        pltpu.SemaphoreType.DMA((rows_out,)),
        pltpu.SemaphoreType.DMA((taken,)),
    ]
    if final:
        out_shape = jax.ShapeDtypeStruct((rows_out, 2 * band - 1, block, block), jnp.bfloat16)
        out_spec = pl.BlockSpec(memory_space=pl.ANY)
        scratch += [
            pltpu.VMEM((rows_out, columns, block, block), jnp.bfloat16),
            pltpu.SemaphoreType.DMA((2, rows_out)),
        ]
    else:
        out_shape = pltpu.VMEM((columns // 2, rows_out * block, 2 * block), kind)
        out_spec = pl.BlockSpec(memory_space=pltpu.VMEM)
    return pl.pallas_call(
        functools.partial(product_kernel, plan),
        out_shape=out_shape,
        in_specs=in_specs,
        out_specs=out_spec,
        scratch_shapes=scratch,
        compiler_params=pltpu.CompilerParams(vmem_limit_bytes=VMEM_LIMIT),
        cost_estimate=pl.CostEstimate(flops=0, bytes_accessed=0, transcendentals=0),
    )(*operands)


def local(a_blocks, b_blocks, a_extent, b_extent):
    rows, band, depth, block = a_blocks.shape
    ring = lax.axis_size("row") * lax.axis_size("col")
    rows_out = rows // lax.axis_size("rep")

    starts = ((rows - EXTRA_ROWS, REST, 0), (0, EXTRA_ROWS, rows - REST))
    sizes = (EXTRA_ROWS, rows - EXTRA_ROWS - REST, REST)
    spans = list(zip(*starts))

    half_band = (band - 1) // 2
    distance = jnp.abs(lax.broadcasted_iota(jnp.int32, b_blocks.shape, 1) - half_band)
    live = distance <= b_extent[:, None, None, None]

    outer = to_outer_neighbour(b_blocks, ring)
    outer_extent = to_outer_neighbour(b_extent, ring)
    b_own = b_blocks * live.astype(b_blocks.dtype)
    across = over_rep(b_blocks)
    peer = to_chip_peer(b_own, ring)
    turned, turned_send = turned_left(a_blocks, a_extent, rows_out)
    turned_across = over_rep(turned_send)
    across = after(across, turned_send, outer_extent)
    *onward, across = picked(across, [*spans[:2], (0, 0)], [*sizes[:2], rows], b_extent)
    across_outer = [to_outer_neighbour(x, ring) for x in onward]
    extra, rest = picked(
        outer, [spans[0], spans[2][::-1]], [sizes[0], sizes[2]], outer_extent
    )
    extra = to_second_neighbour(extra, ring)
    across_outer.append(over_rep(rest))
    across_extra = to_second_neighbour(across_outer[0], ring)
    across_peer = to_chip_peer(across, ring)

    def window_rows(rep_value, core_value):
        sides = ("outer", "peer") if core_value == 0 else ("peer", "outer")
        line = [(kind, i) for kind in (sides[0], "own", sides[1]) for i in range(rows)]
        extra_line = [("extra", i) for i in range(EXTRA_ROWS)]
        return extra_line + line if rep_value == 0 else line + extra_line

    def where_of(index):
        def where(rep_value, core_value):
            found = []
            for slot, (kind, i) in enumerate(window_rows(rep_value, core_value)):
                if kind not in index:
                    continue
                source = index[kind]
                if isinstance(source, tuple):
                    spans = zip(starts[rep_value], sizes)
                    piece = [low <= i < low + size for low, size in spans].index(True)
                    found.append((slot, source[piece], i - starts[rep_value][piece]))
                else:
                    found.append((slot, source, i))
            return found

        return where

    total = partial_product(
        turned,
        [b_own, peer, outer, extra],
        where_of({"own": 0, "peer": 1, "outer": 2, "extra": 3}),
        None,
        rows_out,
        jnp.bfloat16,
        (2, outer_extent),
    )
    total = partial_product(
        turned_across,
        [across, across_peer],
        where_of({"own": 0, "peer": 1}),
        total,
        rows_out,
        jnp.float32,
    )
    return partial_product(
        turned_across,
        [*across_outer, across_extra],
        where_of({"outer": (0, 1, 2), "extra": 3}),
        total,
        rows_out,
        None,
    )


def solution(mesh):
    return jax.shard_map(
        local,
        mesh=mesh,
        in_specs=(
            P(("row", "col"), None, "rep", None),
            P(("row", "col"), None, "rep", None),
            P(("row", "col")),
            P(("row", "col")),
        ),
        out_specs=P(("row", "col", "rep"), None, None, None),
        check_vma=False,
    )
```

```python
import functools

import jax
import jax.numpy as jnp
from jax import lax
from jax.experimental import pallas as pl
from jax.experimental.pallas import tpu as pltpu
from jax.sharding import PartitionSpec as P

RING = ("row", "col")
EVERY = ("row", "col", "rep")
EXTRA_ROWS = 2
REST = 1
VMEM_LIMIT = 24 * 2**20


def to_chip_peer(x, ring):
    return lax.ppermute(x, RING, [(g, g ^ 1) for g in range(ring)])


def to_outer_neighbour(x, ring):
    return lax.ppermute(x, RING, [(g, (g + 2 * (g % 2) - 1) % ring) for g in range(ring)])


def to_second_neighbour(x, ring):
    pairs = []
    for g in range(ring):
        owner = g + 1 if g % 2 else g - 1
        pairs.append((2 * g, 2 * ((owner + 2) % ring)))
        pairs.append((2 * g + 1, 2 * ((owner - 2) % ring) + 1))
    return lax.ppermute(x, EVERY, pairs)


def over_rep(x):
    return lax.ppermute(x, "rep", [(0, 1), (1, 0)])


def turn_kernel(rows_out, extent_ref, a_ref, keep_ref, send_ref):
    rows, band, depth, block = a_ref.shape
    half_band = (band - 1) // 2
    squares = keep_ref.shape[2] // (2 * depth)
    blank = jnp.zeros((depth, block), a_ref.dtype)
    rep = lax.axis_index("rep")

    def turn(row, into_ref):
        shift = first_slot(row // rows_out, row % rows_out) % 2
        extent = extent_ref[row]

        def piece(offset):
            if not 0 <= offset < band:
                return blank
            return jnp.where(abs(offset - half_band) <= extent, a_ref[row, offset], blank)

        for square in range(squares):
            offset = 2 * square - shift
            both = jnp.concatenate([piece(offset), piece(offset + 1)], 0)
            into_ref[row % rows_out, :, square * 2 * depth : (square + 1) * 2 * depth] = both.T

    for rep_value in range(rows // rows_out):

        @pl.when(rep == rep_value)
        def _(rep_value=rep_value):
            for row in range(rows):
                turn(row, keep_ref if row // rows_out == rep_value else send_ref)


def turned_left(a_blocks, a_extent, rows_out):
    rows, band, depth, block = a_blocks.shape
    shape = jax.ShapeDtypeStruct((rows_out, block, (band + 1) * depth), a_blocks.dtype)
    return pl.pallas_call(
        functools.partial(turn_kernel, rows_out),
        out_shape=(shape, shape),
        in_specs=[
            pl.BlockSpec(memory_space=pltpu.SMEM),
            pl.BlockSpec(memory_space=pltpu.VMEM),
        ],
        out_specs=(pl.BlockSpec(memory_space=pltpu.VMEM),) * 2,
        compiler_params=pltpu.CompilerParams(vmem_limit_bytes=8 * 2**20),
        cost_estimate=pl.CostEstimate(flops=0, bytes_accessed=0, transcendentals=0),
    )(a_extent, a_blocks)


def clear_absent(ref, at, extent, band):
    half_band = (band - 1) // 2

    def clear(offset, carry):
        for b in (offset, band - 1 - offset):
            ref[at(b)] = jnp.zeros(ref.shape[-2:], ref.dtype)
        return carry

    lax.fori_loop(0, half_band - extent, clear, 0)


def pick_kernel(spans, masks, *refs):
    refs = list(refs)
    extent_ref = refs.pop(0) if masks else None
    x_ref, out_refs, sem = refs[0], refs[1:-1], refs[-1]
    rep = lax.axis_index("rep")
    starts = [jnp.where(rep == 0, low, high) for low, high in spans]

    def copies():
        return [
            pltpu.make_async_copy(x_ref.at[pl.ds(start, out_ref.shape[0])], out_ref, sem.at[i])
            for i, (start, out_ref) in enumerate(zip(starts, out_refs))
        ]

    for copy in copies():
        copy.start()
    for copy in copies():
        copy.wait()
    if masks:
        for start, out_ref in zip(starts, out_refs):
            for row in range(out_ref.shape[0]):
                clear_absent(
                    out_ref, lambda b, row=row: (row, b), extent_ref[start + row], out_ref.shape[1]
                )


def picked(x, spans, sizes, extents=None):
    masks = extents is not None
    shapes = [jax.ShapeDtypeStruct((size, *x.shape[1:]), x.dtype) for size in sizes]
    out_space = pltpu.VMEM if masks else pl.ANY
    in_specs = [pl.BlockSpec(memory_space=pltpu.SMEM)] if masks else []
    return pl.pallas_call(
        functools.partial(pick_kernel, spans, masks),
        out_shape=shapes,
        in_specs=in_specs + [pl.BlockSpec(memory_space=pl.ANY)],
        out_specs=[pl.BlockSpec(memory_space=out_space)] * len(sizes),
        scratch_shapes=[pltpu.SemaphoreType.DMA((len(sizes),))],
        compiler_params=pltpu.CompilerParams(vmem_limit_bytes=(4 if masks else 1) * 2**20),
        cost_estimate=pl.CostEstimate(flops=0, bytes_accessed=0, transcendentals=0),
    )(*([extents] if masks else []), x)


def after(x, *others):
    return lax.optimization_barrier((x, *others))[0]


def first_slot(rep_value, row):
    return row + rep_value


def product_kernel(plan, *refs):
    refs = list(refs)
    turned_ref = refs.pop(0)
    source_refs = [refs.pop(0) for _ in range(plan["sources"])]
    partial_ref = refs.pop(0) if plan["partial"] else None
    out_ref, left, window, left_sem, row_sem = refs[:5]
    final = plan["final"]
    if final:
        result, out_sem = refs[5:]
    band, rows_out = plan["band"], plan["rows_out"]
    columns, slots, depth, block = window.shape
    pairs = columns // 2
    reach = (band + 1) * depth
    width = slots * depth
    rep = lax.axis_index("rep")
    core = lax.rem(lax.axis_index("col"), 2)

    def left_copy(row, at):
        return pltpu.make_async_copy(
            turned_ref.at[row],
            left.at[pl.ds(row * block, block), pl.ds(at, reach)],
            left_sem.at[row],
        )

    def row_copy(source, position, slot, index):
        return pltpu.make_async_copy(
            source.at[position], window.at[pl.ds(slot, band), slot], row_sem.at[index]
        )

    def out_copy(half, row):
        low = half * (band - 1)
        count = band - 1 if half == 0 else band
        return pltpu.make_async_copy(
            result.at[row, pl.ds(first_slot(rep, row) + low, count)],
            out_ref.at[row, pl.ds(low, count)],
            out_sem.at[half, row],
        )

    def place_left(rep_value):
        for row in range(rows_out):
            at = first_slot(rep_value, row) // 2 * 2 * depth
            left_copy(row, at).start()
            lines = slice(row * block, (row + 1) * block)
            if at:
                left[lines, :at] = jnp.zeros((block, at), left.dtype)
            if at + reach < width:
                left[lines, at + reach :] = jnp.zeros((block, width - at - reach), left.dtype)

    def place_rows(listed):
        for index, (slot, source, position) in enumerate(listed):
            row_copy(source_refs[source], position, slot, index).start()
        blank = jnp.zeros((depth, block), window.dtype)
        taken = {slot for slot, _, _ in listed}
        for pair in range(pairs):
            if 2 * pair + 1 in taken:
                window[2 * pair, 2 * pair + 1] = blank
            if 2 * pair + 1 - band in taken:
                window[2 * pair + 1, 2 * pair + 1 - band] = blank

    def multiply(ranges, some_pairs):
        for pair in some_pairs:
            total = None
            for low, high in ranges:
                first, last = max(low, 2 * pair + 1 - band), min(high, 2 * pair + 2)
                if first >= last:
                    continue
                span = (last - first) * depth
                right = jnp.concatenate(
                    [
                        window[2 * pair + side, first:last].reshape(span, block)
                        for side in range(2)
                    ],
                    1,
                )
                term = jnp.dot(
                    left[:, first * depth : last * depth],
                    right,
                    preferred_element_type=jnp.float32,
                )
                total = term if total is None else total + term
            if partial_ref is not None:
                before = partial_ref[pair].astype(jnp.float32)
                total = before if total is None else total + before
            if not final:
                out_ref[pair] = total.astype(out_ref.dtype)
                continue
            total = total.astype(result.dtype)
            for row in range(rows_out):
                for side in range(2):
                    result[row, 2 * pair + side] = total[
                        row * block : (row + 1) * block, side * block : (side + 1) * block
                    ]

    for rep_value in range(2):

        @pl.when(rep == rep_value)
        def _(rep_value=rep_value):
            place_left(rep_value)

        for core_value in range(2):

            @pl.when((rep == rep_value) & (core == core_value))
            def _(rep_value=rep_value, core_value=core_value):
                place_rows(plan["where"](rep_value, core_value))

    for row in range(rows_out):
        left_copy(row, 0).wait()
    for index in range(plan["taken"]):
        row_copy(source_refs[0], 0, 0, index).wait()
    parts = [range(pairs)]
    if final:
        middle = (band - 1 + rows_out) // 2 + 1
        parts = [range(middle), range(middle, pairs)]
    for half, part in enumerate(parts):
        if plan["taken"] == slots:
            multiply([(0, slots)], part)
        else:
            for rep_value in range(2):
                for core_value in range(2):

                    @pl.when((rep == rep_value) & (core == core_value))
                    def _(rep_value=rep_value, core_value=core_value, part=part):
                        taken = sorted(slot for slot, _, _ in plan["where"](rep_value, core_value))
                        lows = [slot for slot in taken if slot - 1 not in taken]
                        highs = [slot + 1 for slot in taken if slot + 1 not in taken]
                        multiply(list(zip(lows, highs)), part)

        if final:
            for row in range(rows_out):
                out_copy(half, row).start()
    if final:
        for half in range(2):
            for row in range(rows_out):
                out_copy(half, row).wait()


def partial_product(turned, sources, where, partial, rows_out, kind):
    band, depth, block = sources[0].shape[1:]
    slots = rows_out + band
    columns = slots + band - 1
    taken = len(where(0, 0))
    final = kind is None
    plan = {
        "sources": len(sources),
        "where": where,
        "taken": taken,
        "band": band,
        "rows_out": rows_out,
        "partial": partial is not None,
        "final": final,
    }
    operands = [turned, *sources]
    in_specs = [pl.BlockSpec(memory_space=pl.ANY)] * len(operands)
    if partial is not None:
        operands.append(partial)
        in_specs.append(pl.BlockSpec(memory_space=pltpu.VMEM))
    scratch = [
        pltpu.VMEM((rows_out * block, slots * depth), jnp.bfloat16),
        pltpu.VMEM((columns, slots, depth, block), jnp.bfloat16),
        pltpu.SemaphoreType.DMA((rows_out,)),
        pltpu.SemaphoreType.DMA((taken,)),
    ]
    if final:
        out_shape = jax.ShapeDtypeStruct((rows_out, 2 * band - 1, block, block), jnp.bfloat16)
        out_spec = pl.BlockSpec(memory_space=pl.ANY)
        scratch += [
            pltpu.VMEM((rows_out, columns, block, block), jnp.bfloat16),
            pltpu.SemaphoreType.DMA((2, rows_out)),
        ]
    else:
        out_shape = pltpu.VMEM((columns // 2, rows_out * block, 2 * block), kind)
        out_spec = pl.BlockSpec(memory_space=pltpu.VMEM)
    return pl.pallas_call(
        functools.partial(product_kernel, plan),
        out_shape=out_shape,
        in_specs=in_specs,
        out_specs=out_spec,
        scratch_shapes=scratch,
        compiler_params=pltpu.CompilerParams(vmem_limit_bytes=VMEM_LIMIT),
        cost_estimate=pl.CostEstimate(flops=0, bytes_accessed=0, transcendentals=0),
    )(*operands)


def local(a_blocks, b_blocks, a_extent, b_extent):
    rows, band, depth, block = a_blocks.shape
    ring = lax.axis_size("row") * lax.axis_size("col")
    rows_out = rows // lax.axis_size("rep")

    starts = ((rows - EXTRA_ROWS, REST, 0), (0, EXTRA_ROWS, rows - REST))
    sizes = (EXTRA_ROWS, rows - EXTRA_ROWS - REST, REST)
    spans = list(zip(*starts))

    half_band = (band - 1) // 2
    distance = jnp.abs(lax.broadcasted_iota(jnp.int32, b_blocks.shape, 1) - half_band)
    live = distance <= b_extent[:, None, None, None]

    b_own = b_blocks * live.astype(b_blocks.dtype)
    outer = to_outer_neighbour(b_own, ring)
    across = over_rep(b_blocks)
    peer = to_chip_peer(b_own, ring)
    turned, turned_send = turned_left(a_blocks, a_extent, rows_out)
    turned_across = over_rep(turned_send)
    across = after(across, turned_send)
    *onward, across = picked(across, [*spans[:2], (0, 0)], [*sizes[:2], rows], b_extent)
    across_outer = [to_outer_neighbour(x, ring) for x in onward]
    extra, rest = picked(outer, [spans[0], spans[2][::-1]], [sizes[0], sizes[2]])
    extra = to_second_neighbour(extra, ring)
    across_outer.append(over_rep(rest))
    across_extra = to_second_neighbour(across_outer[0], ring)
    across_peer = to_chip_peer(across, ring)

    def window_rows(rep_value, core_value):
        sides = ("outer", "peer") if core_value == 0 else ("peer", "outer")
        line = [(kind, i) for kind in (sides[0], "own", sides[1]) for i in range(rows)]
        extra_line = [("extra", i) for i in range(EXTRA_ROWS)]
        return extra_line + line if rep_value == 0 else line + extra_line

    def where_of(index):
        def where(rep_value, core_value):
            found = []
            for slot, (kind, i) in enumerate(window_rows(rep_value, core_value)):
                if kind not in index:
                    continue
                source = index[kind]
                if isinstance(source, tuple):
                    spans = zip(starts[rep_value], sizes)
                    piece = [low <= i < low + size for low, size in spans].index(True)
                    found.append((slot, source[piece], i - starts[rep_value][piece]))
                else:
                    found.append((slot, source, i))
            return found

        return where

    total = partial_product(
        turned,
        [b_own, peer, outer, extra],
        where_of({"own": 0, "peer": 1, "outer": 2, "extra": 3}),
        None,
        rows_out,
        jnp.bfloat16,
    )
    total = partial_product(
        turned_across,
        [across, across_peer],
        where_of({"own": 0, "peer": 1}),
        total,
        rows_out,
        jnp.float32,
    )
    return partial_product(
        turned_across,
        [*across_outer, across_extra],
        where_of({"outer": (0, 1, 2), "extra": 3}),
        total,
        rows_out,
        None,
    )


def solution(mesh):
    return jax.shard_map(
        local,
        mesh=mesh,
        in_specs=(
            P(("row", "col"), None, "rep", None),
            P(("row", "col"), None, "rep", None),
            P(("row", "col")),
            P(("row", "col")),
        ),
        out_specs=P(("row", "col", "rep"), None, None, None),
        check_vma=False,
    )
```

```python
import functools

import jax
import jax.numpy as jnp
from jax import lax
from jax.experimental import pallas as pl
from jax.experimental.pallas import tpu as pltpu
from jax.sharding import PartitionSpec as P

RING = ("row", "col")
EVERY = ("row", "col", "rep")
EXTRA_ROWS = 2
PEER_ROWS = 2
REST = 1
VMEM_LIMIT = 24 * 2**20


def to_chip_peer(x, ring):
    return lax.ppermute(x, RING, [(g, g ^ 1) for g in range(ring)])


def to_outer_neighbour(x, ring):
    return lax.ppermute(x, RING, [(g, (g + 2 * (g % 2) - 1) % ring) for g in range(ring)])


def to_second_neighbour(x, ring):
    pairs = []
    for g in range(ring):
        owner = g + 1 if g % 2 else g - 1
        pairs.append((2 * g, 2 * ((owner + 2) % ring)))
        pairs.append((2 * g + 1, 2 * ((owner - 2) % ring) + 1))
    return lax.ppermute(x, EVERY, pairs)


def over_rep(x):
    return lax.ppermute(x, "rep", [(0, 1), (1, 0)])


def turn_kernel(rows_out, extent_ref, a_ref, keep_ref, send_ref):
    rows, band, depth, block = a_ref.shape
    half_band = (band - 1) // 2
    squares = keep_ref.shape[2] // (2 * depth)
    blank = jnp.zeros((depth, block), a_ref.dtype)
    rep = lax.axis_index("rep")

    def turn(row, into_ref):
        shift = first_slot(row // rows_out, row % rows_out) % 2
        extent = extent_ref[row]

        def piece(offset):
            if not 0 <= offset < band:
                return blank
            return jnp.where(abs(offset - half_band) <= extent, a_ref[row, offset], blank)

        for square in range(squares):
            offset = 2 * square - shift
            both = jnp.concatenate([piece(offset), piece(offset + 1)], 0)
            into_ref[row % rows_out, :, square * 2 * depth : (square + 1) * 2 * depth] = both.T

    for rep_value in range(rows // rows_out):

        @pl.when(rep == rep_value)
        def _(rep_value=rep_value):
            for row in range(rows):
                turn(row, keep_ref if row // rows_out == rep_value else send_ref)


def turned_left(a_blocks, a_extent, rows_out):
    rows, band, depth, block = a_blocks.shape
    shape = jax.ShapeDtypeStruct((rows_out, block, (band + 1) * depth), a_blocks.dtype)
    return pl.pallas_call(
        functools.partial(turn_kernel, rows_out),
        out_shape=(shape, shape),
        in_specs=[
            pl.BlockSpec(memory_space=pltpu.SMEM),
            pl.BlockSpec(memory_space=pltpu.VMEM),
        ],
        out_specs=(pl.BlockSpec(memory_space=pltpu.VMEM),) * 2,
        compiler_params=pltpu.CompilerParams(vmem_limit_bytes=8 * 2**20),
        cost_estimate=pl.CostEstimate(flops=0, bytes_accessed=0, transcendentals=0),
    )(a_extent, a_blocks)


def pick_kernel(band, spans, masks, *refs):
    refs = list(refs)
    extent_ref = refs.pop(0) if masks else None
    x_ref, out_refs, sem = refs[0], refs[1:-1], refs[-1]
    half_band = (band - 1) // 2
    rep = lax.axis_index("rep")

    def copies():
        return [
            pltpu.make_async_copy(
                x_ref.at[pl.ds(jnp.where(rep == 0, low, high), out_ref.shape[0])],
                out_ref,
                sem.at[i],
            )
            for i, ((low, high), out_ref) in enumerate(zip(spans, out_refs))
        ]

    def clear_row(out_ref, at, low, high, extent):
        def clear(offset, carry):
            if low <= 0:
                out_ref[at + offset] = jnp.zeros(out_ref.shape[1:], out_ref.dtype)
            if high >= band:
                out_ref[at + band - 1 - offset] = jnp.zeros(out_ref.shape[1:], out_ref.dtype)
            return carry

        lax.fori_loop(0, half_band - extent, clear, 0)

    for copy in copies():
        copy.start()
    for copy in copies():
        copy.wait()
    if not masks:
        return
    for rep_value in range(2):

        @pl.when(rep == rep_value)
        def _(rep_value=rep_value):
            for span, out_ref in zip(spans, out_refs):
                start = span[rep_value]
                end = start + out_ref.shape[0]
                for row in range(start // band, (end + band - 1) // band):
                    at = row * band - start
                    clear_row(out_ref, at, max(-at, 0), min(end - start - at, band), extent_ref[row])


def picked(x, spans, sizes, extents=None):
    rows, band, depth, block = x.shape
    masks = extents is not None
    shapes = [jax.ShapeDtypeStruct((size, depth, block), x.dtype) for size in sizes]
    out_space = pltpu.VMEM if masks else pl.ANY
    in_specs = [pl.BlockSpec(memory_space=pltpu.SMEM)] if masks else []
    return pl.pallas_call(
        functools.partial(pick_kernel, band, spans, masks),
        out_shape=shapes,
        in_specs=in_specs + [pl.BlockSpec(memory_space=pl.ANY)],
        out_specs=[pl.BlockSpec(memory_space=out_space)] * len(sizes),
        scratch_shapes=[pltpu.SemaphoreType.DMA((len(sizes),))],
        compiler_params=pltpu.CompilerParams(vmem_limit_bytes=(4 if masks else 1) * 2**20),
        cost_estimate=pl.CostEstimate(flops=0, bytes_accessed=0, transcendentals=0),
    )(*([extents] if masks else []), x.reshape(rows * band, depth, block))


def after(x, *others):
    return lax.optimization_barrier((x, *others))[0]


def first_slot(rep_value, row):
    return row + rep_value


def product_kernel(plan, *refs):
    refs = list(refs)
    turned_ref = refs.pop(0)
    source_refs = [refs.pop(0) for _ in range(plan["sources"])]
    partial_ref = refs.pop(0) if plan["partial"] else None
    out_ref, left, window, left_sem, row_sem = refs[:5]
    final = plan["final"]
    if final:
        result, out_sem = refs[5:]
    band, rows_out = plan["band"], plan["rows_out"]
    columns, slots, depth, block = window.shape
    pairs = columns // 2
    reach = (band + 1) * depth
    width = slots * depth
    rep = lax.axis_index("rep")
    core = lax.rem(lax.axis_index("col"), 2)

    def left_copy(row, at):
        return pltpu.make_async_copy(
            turned_ref.at[row],
            left.at[pl.ds(row * block, block), pl.ds(at, reach)],
            left_sem.at[row],
        )

    def row_copy(source, at, slot, first, count, index):
        return pltpu.make_async_copy(
            source.at[pl.ds(at, count)],
            window.at[pl.ds(slot + first, count), slot],
            row_sem.at[index],
        )

    def out_copy(half, row):
        low = half * (band - 1)
        count = band - 1 if half == 0 else band
        return pltpu.make_async_copy(
            result.at[row, pl.ds(first_slot(rep, row) + low, count)],
            out_ref.at[row, pl.ds(low, count)],
            out_sem.at[half, row],
        )

    def place_left(rep_value):
        for row in range(rows_out):
            at = first_slot(rep_value, row) // 2 * 2 * depth
            left_copy(row, at).start()
            lines = slice(row * block, (row + 1) * block)
            if at:
                left[lines, :at] = jnp.zeros((block, at), left.dtype)
            if at + reach < width:
                left[lines, at + reach :] = jnp.zeros((block, width - at - reach), left.dtype)

    def place_rows(listed):
        for index, (slot, source, at, first, count) in enumerate(listed):
            row_copy(source_refs[source], at, slot, first, count, index).start()
        blank = jnp.zeros((depth, block), window.dtype)
        taken = {slot for slot, *_ in listed}
        for pair in range(pairs):
            if 2 * pair + 1 in taken:
                window[2 * pair, 2 * pair + 1] = blank
            if 2 * pair + 1 - band in taken:
                window[2 * pair + 1, 2 * pair + 1 - band] = blank

    def multiply(ranges, some_pairs):
        for pair in some_pairs:
            total = None
            for low, high in ranges:
                first, last = max(low, 2 * pair + 1 - band), min(high, 2 * pair + 2)
                if first >= last:
                    continue
                span = (last - first) * depth
                right = jnp.concatenate(
                    [
                        window[2 * pair + side, first:last].reshape(span, block)
                        for side in range(2)
                    ],
                    1,
                )
                term = jnp.dot(
                    left[:, first * depth : last * depth],
                    right,
                    preferred_element_type=jnp.float32,
                )
                total = term if total is None else total + term
            if partial_ref is not None:
                before = partial_ref[pair].astype(jnp.float32)
                total = before if total is None else total + before
            if not final:
                out_ref[pair] = total.astype(out_ref.dtype)
                continue
            total = total.astype(result.dtype)
            for row in range(rows_out):
                for side in range(2):
                    result[row, 2 * pair + side] = total[
                        row * block : (row + 1) * block, side * block : (side + 1) * block
                    ]

    for rep_value in range(2):

        @pl.when(rep == rep_value)
        def _(rep_value=rep_value):
            place_left(rep_value)

        for core_value in range(2):

            @pl.when((rep == rep_value) & (core == core_value))
            def _(rep_value=rep_value, core_value=core_value):
                place_rows(plan["where"](rep_value, core_value))

    for row in range(rows_out):
        left_copy(row, 0).wait()
    for index, count in enumerate(plan["counts"]):
        row_copy(source_refs[0], 0, 0, 0, count, index).wait()
    parts = [range(pairs)]
    if final:
        middle = (band - 1 + rows_out) // 2 + 1
        parts = [range(middle), range(middle, pairs)]
    for half, part in enumerate(parts):
        if len(plan["counts"]) == slots:
            multiply([(0, slots)], part)
        else:
            for rep_value in range(2):
                for core_value in range(2):

                    @pl.when((rep == rep_value) & (core == core_value))
                    def _(rep_value=rep_value, core_value=core_value, part=part):
                        taken = sorted({slot for slot, *_ in plan["where"](rep_value, core_value)})
                        lows = [slot for slot in taken if slot - 1 not in taken]
                        highs = [slot + 1 for slot in taken if slot + 1 not in taken]
                        multiply(list(zip(lows, highs)), part)

        if final:
            for row in range(rows_out):
                out_copy(half, row).start()
    if final:
        for half in range(2):
            for row in range(rows_out):
                out_copy(half, row).wait()


def partial_product(turned, sources, where, partial, rows_out, band, kind):
    depth, block = sources[0].shape[1:]
    slots = rows_out + band
    columns = slots + band - 1
    counts = [count for *_, count in where(0, 0)]
    final = kind is None
    plan = {
        "sources": len(sources),
        "where": where,
        "counts": counts,
        "band": band,
        "rows_out": rows_out,
        "partial": partial is not None,
        "final": final,
    }
    operands = [turned, *sources]
    in_specs = [pl.BlockSpec(memory_space=pl.ANY)] * len(operands)
    if partial is not None:
        operands.append(partial)
        in_specs.append(pl.BlockSpec(memory_space=pltpu.VMEM))
    scratch = [
        pltpu.VMEM((rows_out * block, slots * depth), jnp.bfloat16),
        pltpu.VMEM((columns, slots, depth, block), jnp.bfloat16),
        pltpu.SemaphoreType.DMA((rows_out,)),
        pltpu.SemaphoreType.DMA((len(counts),)),
    ]
    if final:
        out_shape = jax.ShapeDtypeStruct((rows_out, 2 * band - 1, block, block), jnp.bfloat16)
        out_spec = pl.BlockSpec(memory_space=pl.ANY)
        scratch += [
            pltpu.VMEM((rows_out, columns, block, block), jnp.bfloat16),
            pltpu.SemaphoreType.DMA((2, rows_out)),
        ]
    else:
        out_shape = pltpu.VMEM((columns // 2, rows_out * block, 2 * block), kind)
        out_spec = pl.BlockSpec(memory_space=pltpu.VMEM)
    return pl.pallas_call(
        functools.partial(product_kernel, plan),
        out_shape=out_shape,
        in_specs=in_specs,
        out_specs=out_spec,
        scratch_shapes=scratch,
        compiler_params=pltpu.CompilerParams(vmem_limit_bytes=VMEM_LIMIT),
        cost_estimate=pl.CostEstimate(flops=0, bytes_accessed=0, transcendentals=0),
    )(*operands)


def local(a_blocks, b_blocks, a_extent, b_extent):
    rows, band, depth, block = a_blocks.shape
    ring = lax.axis_size("row") * lax.axis_size("col")
    rows_out = rows // lax.axis_size("rep")
    half_band = (band - 1) // 2

    def flat(x):
        return x.reshape(-1, depth, block)

    extra_size, rest_size = EXTRA_ROWS * band, REST * band + half_band
    sizes = (extra_size, rows * band - extra_size - rest_size, rest_size)
    starts = ((rows * band - extra_size, rest_size, 0), (0, extra_size, rows * band - rest_size))
    spans = list(zip(*starts))

    distance = jnp.abs(lax.broadcasted_iota(jnp.int32, b_blocks.shape, 1) - half_band)
    live = distance <= b_extent[:, None, None, None]
    b_own = b_blocks * live.astype(b_blocks.dtype)
    outer = to_outer_neighbour(b_own, ring)
    across = over_rep(b_blocks)
    peer = to_chip_peer(b_own, ring)
    turned, turned_send = turned_left(a_blocks, a_extent, rows_out)
    turned_across = over_rep(turned_send)
    across = after(across, turned_send)
    parts = tuple(i * PEER_ROWS * band for i in range(rows // PEER_ROWS))
    part_sizes = (PEER_ROWS * band,) * len(parts)
    picks = picked(across, [*spans[:2], *zip(parts, parts)], [*sizes[:2], *part_sizes], b_extent)
    onward, across_own = picks[:2], picks[2:]
    across_outer = [to_outer_neighbour(x, ring) for x in onward]
    extra, rest = picked(after(outer, peer), [spans[0], spans[2][::-1]], [sizes[0], sizes[2]])
    extra = to_second_neighbour(extra, ring)
    across_outer.append(over_rep(rest))
    across_extra = to_second_neighbour(across_outer[0], ring)
    across_peer = [
        to_chip_peer(x if i == 0 else after(x, across_outer[0]), ring)
        for i, x in enumerate(across_own)
    ]

    def window_rows(rep_value, core_value):
        sides = ("outer", "peer") if core_value == 0 else ("peer", "outer")
        line = [(kind, i) for kind in (sides[0], "own", sides[1]) for i in range(rows)]
        extra_line = [("extra", i) for i in range(EXTRA_ROWS)]
        return extra_line + line if rep_value == 0 else line + extra_line

    def where_of(index):
        def where(rep_value, core_value):
            found = []
            for slot, (kind, i) in enumerate(window_rows(rep_value, core_value)):
                if kind not in index:
                    continue
                sources, lows, counts = index[kind]
                for source, low, count in zip(sources, lows[rep_value], counts):
                    first = max(i * band, low)
                    last = min((i + 1) * band, low + count)
                    if first < last:
                        found.append((slot, source, first - low, first - i * band, last - first))
            return sorted(found, key=lambda piece: -piece[-1])

        return where

    whole = ((0,), (0,)), (rows * band,)
    only_extra = ((0,), (0,)), (extra_size,)
    thirds = (parts, parts), part_sizes
    count = len(parts)
    total = partial_product(
        turned,
        [flat(b_own), flat(peer), flat(outer), extra],
        where_of(
            {
                "own": ((0,), *whole),
                "peer": ((1,), *whole),
                "outer": ((2,), *whole),
                "extra": ((3,), *only_extra),
            }
        ),
        None,
        rows_out,
        band,
        jnp.bfloat16,
    )
    total = partial_product(
        turned_across,
        [*across_own, *across_peer],
        where_of(
            {"own": (range(count), *thirds), "peer": (range(count, 2 * count), *thirds)}
        ),
        total,
        rows_out,
        band,
        jnp.float32,
    )
    return partial_product(
        turned_across,
        [*across_outer, across_extra],
        where_of({"outer": ((0, 1, 2), starts, sizes), "extra": ((3,), *only_extra)}),
        total,
        rows_out,
        band,
        None,
    )


def solution(mesh):
    return jax.shard_map(
        local,
        mesh=mesh,
        in_specs=(
            P(("row", "col"), None, "rep", None),
            P(("row", "col"), None, "rep", None),
            P(("row", "col")),
            P(("row", "col")),
        ),
        out_specs=P(("row", "col", "rep"), None, None, None),
        check_vma=False,
    )
```

```python
import functools

import jax
import jax.numpy as jnp
from jax import lax
from jax.experimental import pallas as pl
from jax.experimental.pallas import tpu as pltpu
from jax.sharding import PartitionSpec as P

RING = ("row", "col")
EVERY = ("row", "col", "rep")
EXTRA_ROWS = 2
EARLY_PEER_ROWS = 4
OUT_PARTS = 3
REST = 1
VMEM_LIMIT = 24 * 2**20


def to_chip_peer(x, ring):
    return lax.ppermute(x, RING, [(g, g ^ 1) for g in range(ring)])


def to_outer_neighbour(x, ring):
    return lax.ppermute(x, RING, [(g, (g + 2 * (g % 2) - 1) % ring) for g in range(ring)])


def to_second_neighbour(x, ring):
    pairs = []
    for g in range(ring):
        owner = g + 1 if g % 2 else g - 1
        pairs.append((2 * g, 2 * ((owner + 2) % ring)))
        pairs.append((2 * g + 1, 2 * ((owner - 2) % ring) + 1))
    return lax.ppermute(x, EVERY, pairs)


def over_rep(x):
    return lax.ppermute(x, "rep", [(0, 1), (1, 0)])


def turn_kernel(rows_out, extent_ref, a_ref, keep_ref, send_ref):
    rows, band, depth, block = a_ref.shape
    half_band = (band - 1) // 2
    squares = keep_ref.shape[2] // (2 * depth)
    blank = jnp.zeros((depth, block), a_ref.dtype)
    rep = lax.axis_index("rep")

    def turn(row, into_ref):
        shift = first_slot(row // rows_out, row % rows_out) % 2
        extent = extent_ref[row]

        def piece(offset):
            if not 0 <= offset < band:
                return blank
            return jnp.where(abs(offset - half_band) <= extent, a_ref[row, offset], blank)

        for square in range(squares):
            offset = 2 * square - shift
            both = jnp.concatenate([piece(offset), piece(offset + 1)], 0)
            into_ref[row % rows_out, :, square * 2 * depth : (square + 1) * 2 * depth] = both.T

    for rep_value in range(rows // rows_out):

        @pl.when(rep == rep_value)
        def _(rep_value=rep_value):
            for row in range(rows):
                turn(row, keep_ref if row // rows_out == rep_value else send_ref)


def turned_left(a_blocks, a_extent, rows_out):
    rows, band, depth, block = a_blocks.shape
    shape = jax.ShapeDtypeStruct((rows_out, block, (band + 1) * depth), a_blocks.dtype)
    return pl.pallas_call(
        functools.partial(turn_kernel, rows_out),
        out_shape=(shape, shape),
        in_specs=[
            pl.BlockSpec(memory_space=pltpu.SMEM),
            pl.BlockSpec(memory_space=pltpu.VMEM),
        ],
        out_specs=(pl.BlockSpec(memory_space=pltpu.VMEM),) * 2,
        compiler_params=pltpu.CompilerParams(vmem_limit_bytes=8 * 2**20),
        cost_estimate=pl.CostEstimate(flops=0, bytes_accessed=0, transcendentals=0),
    )(a_extent, a_blocks)


def pick_kernel(band, spans, masks, *refs):
    refs = list(refs)
    extent_ref = refs.pop(0) if masks else None
    x_ref, out_refs, sem = refs[0], refs[1:-1], refs[-1]
    half_band = (band - 1) // 2
    rep = lax.axis_index("rep")

    def copies():
        return [
            pltpu.make_async_copy(
                x_ref.at[pl.ds(jnp.where(rep == 0, low, high), out_ref.shape[0])],
                out_ref,
                sem.at[i],
            )
            for i, ((low, high), out_ref) in enumerate(zip(spans, out_refs))
        ]

    def clear_row(out_ref, at, low, high, extent):
        def clear(offset, carry):
            if low <= 0:
                out_ref[at + offset] = jnp.zeros(out_ref.shape[1:], out_ref.dtype)
            if high >= band:
                out_ref[at + band - 1 - offset] = jnp.zeros(out_ref.shape[1:], out_ref.dtype)
            return carry

        lax.fori_loop(0, half_band - extent, clear, 0)

    for copy in copies():
        copy.start()
    for copy in copies():
        copy.wait()
    if not masks:
        return
    for rep_value in range(2):

        @pl.when(rep == rep_value)
        def _(rep_value=rep_value):
            for span, out_ref in zip(spans, out_refs):
                start = span[rep_value]
                end = start + out_ref.shape[0]
                for row in range(start // band, (end + band - 1) // band):
                    at = row * band - start
                    clear_row(out_ref, at, max(-at, 0), min(end - start - at, band), extent_ref[row])


def picked(x, spans, sizes, extents=None):
    rows, band, depth, block = x.shape
    masks = extents is not None
    shapes = [jax.ShapeDtypeStruct((size, depth, block), x.dtype) for size in sizes]
    out_space = pltpu.VMEM if masks else pl.ANY
    in_specs = [pl.BlockSpec(memory_space=pltpu.SMEM)] if masks else []
    return pl.pallas_call(
        functools.partial(pick_kernel, band, spans, masks),
        out_shape=shapes,
        in_specs=in_specs + [pl.BlockSpec(memory_space=pl.ANY)],
        out_specs=[pl.BlockSpec(memory_space=out_space)] * len(sizes),
        scratch_shapes=[pltpu.SemaphoreType.DMA((len(sizes),))],
        compiler_params=pltpu.CompilerParams(vmem_limit_bytes=(4 if masks else 1) * 2**20),
        cost_estimate=pl.CostEstimate(flops=0, bytes_accessed=0, transcendentals=0),
    )(*([extents] if masks else []), x.reshape(rows * band, depth, block))


def after(x, *others):
    return lax.optimization_barrier((x, *others))[0]


def first_slot(rep_value, row):
    return row + rep_value


def product_kernel(plan, *refs):
    refs = list(refs)
    turned_ref = refs.pop(0)
    source_refs = [refs.pop(0) for _ in range(plan["sources"])]
    partial_ref = refs.pop(0) if plan["partial"] else None
    out_ref, left, window, left_sem, row_sem = refs[:5]
    final = plan["final"]
    if final:
        result, out_sem = refs[5:]
    band, rows_out = plan["band"], plan["rows_out"]
    columns, slots, depth, block = window.shape
    pairs = columns // 2
    reach = (band + 1) * depth
    width = slots * depth
    rep = lax.axis_index("rep")
    core = lax.rem(lax.axis_index("col"), 2)

    def left_copy(row, at):
        return pltpu.make_async_copy(
            turned_ref.at[row],
            left.at[pl.ds(row * block, block), pl.ds(at, reach)],
            left_sem.at[row],
        )

    def row_copy(source, at, slot, first, count, index):
        return pltpu.make_async_copy(
            source.at[pl.ds(at, count)],
            window.at[pl.ds(slot + first, count), slot],
            row_sem.at[index],
        )

    bounds = [(2 * band - 1) * i // OUT_PARTS for i in range(OUT_PARTS + 1)]

    def out_copy(part, row):
        low = bounds[part]
        count = bounds[part + 1] - low
        return pltpu.make_async_copy(
            result.at[row, pl.ds(first_slot(rep, row) + low, count)],
            out_ref.at[row, pl.ds(low, count)],
            out_sem.at[part, row],
        )

    def place_left(rep_value):
        for row in range(rows_out):
            at = first_slot(rep_value, row) // 2 * 2 * depth
            left_copy(row, at).start()
            lines = slice(row * block, (row + 1) * block)
            if at:
                left[lines, :at] = jnp.zeros((block, at), left.dtype)
            if at + reach < width:
                left[lines, at + reach :] = jnp.zeros((block, width - at - reach), left.dtype)

    def place_rows(listed):
        for index, (slot, source, at, first, count) in enumerate(listed):
            row_copy(source_refs[source], at, slot, first, count, index).start()
        blank = jnp.zeros((depth, block), window.dtype)
        taken = {slot for slot, *_ in listed}
        for pair in range(pairs):
            if 2 * pair + 1 in taken:
                window[2 * pair, 2 * pair + 1] = blank
            if 2 * pair + 1 - band in taken:
                window[2 * pair + 1, 2 * pair + 1 - band] = blank

    def multiply(ranges, some_pairs):
        for pair in some_pairs:
            total = None
            for low, high in ranges:
                first, last = max(low, 2 * pair + 1 - band), min(high, 2 * pair + 2)
                if first >= last:
                    continue
                span = (last - first) * depth
                right = jnp.concatenate(
                    [
                        window[2 * pair + side, first:last].reshape(span, block)
                        for side in range(2)
                    ],
                    1,
                )
                term = jnp.dot(
                    left[:, first * depth : last * depth],
                    right,
                    preferred_element_type=jnp.float32,
                )
                total = term if total is None else total + term
            if partial_ref is not None:
                before = partial_ref[pair].astype(jnp.float32)
                total = before if total is None else total + before
            if not final:
                out_ref[pair] = total.astype(out_ref.dtype)
                continue
            total = total.astype(result.dtype)
            for row in range(rows_out):
                for side in range(2):
                    result[row, 2 * pair + side] = total[
                        row * block : (row + 1) * block, side * block : (side + 1) * block
                    ]

    for rep_value in range(2):

        @pl.when(rep == rep_value)
        def _(rep_value=rep_value):
            place_left(rep_value)

        for core_value in range(2):

            @pl.when((rep == rep_value) & (core == core_value))
            def _(rep_value=rep_value, core_value=core_value):
                place_rows(plan["where"](rep_value, core_value))

    for row in range(rows_out):
        left_copy(row, 0).wait()
    for index, count in enumerate(plan["counts"]):
        row_copy(source_refs[0], 0, 0, 0, count, index).wait()
    parts = [range(pairs)]
    if final:
        ends = [0, *((bound - 1 + rows_out) // 2 + 1 for bound in bounds[1:-1]), pairs]
        parts = [range(low, high) for low, high in zip(ends, ends[1:])]
    for part, some_pairs in enumerate(parts):
        if len(plan["counts"]) == slots:
            multiply([(0, slots)], some_pairs)
        else:
            for rep_value in range(2):
                for core_value in range(2):

                    @pl.when((rep == rep_value) & (core == core_value))
                    def _(rep_value=rep_value, core_value=core_value, some_pairs=some_pairs):
                        taken = sorted({slot for slot, *_ in plan["where"](rep_value, core_value)})
                        lows = [slot for slot in taken if slot - 1 not in taken]
                        highs = [slot + 1 for slot in taken if slot + 1 not in taken]
                        multiply(list(zip(lows, highs)), some_pairs)

        if final:
            for row in range(rows_out):
                out_copy(part, row).start()
    if final:
        for part in range(OUT_PARTS):
            for row in range(rows_out):
                out_copy(part, row).wait()


def partial_product(turned, sources, where, partial, rows_out, band, kind):
    depth, block = sources[0].shape[1:]
    slots = rows_out + band
    columns = slots + band - 1
    counts = [count for *_, count in where(0, 0)]
    final = kind is None
    plan = {
        "sources": len(sources),
        "where": where,
        "counts": counts,
        "band": band,
        "rows_out": rows_out,
        "partial": partial is not None,
        "final": final,
    }
    operands = [turned, *sources]
    in_specs = [pl.BlockSpec(memory_space=pl.ANY)] * len(operands)
    if partial is not None:
        operands.append(partial)
        in_specs.append(pl.BlockSpec(memory_space=pltpu.VMEM))
    scratch = [
        pltpu.VMEM((rows_out * block, slots * depth), jnp.bfloat16),
        pltpu.VMEM((columns, slots, depth, block), jnp.bfloat16),
        pltpu.SemaphoreType.DMA((rows_out,)),
        pltpu.SemaphoreType.DMA((len(counts),)),
    ]
    if final:
        out_shape = jax.ShapeDtypeStruct((rows_out, 2 * band - 1, block, block), jnp.bfloat16)
        out_spec = pl.BlockSpec(memory_space=pl.ANY)
        scratch += [
            pltpu.VMEM((rows_out, columns, block, block), jnp.bfloat16),
            pltpu.SemaphoreType.DMA((OUT_PARTS, rows_out)),
        ]
    else:
        out_shape = pltpu.VMEM((columns // 2, rows_out * block, 2 * block), kind)
        out_spec = pl.BlockSpec(memory_space=pltpu.VMEM)
    return pl.pallas_call(
        functools.partial(product_kernel, plan),
        out_shape=out_shape,
        in_specs=in_specs,
        out_specs=out_spec,
        scratch_shapes=scratch,
        compiler_params=pltpu.CompilerParams(vmem_limit_bytes=VMEM_LIMIT),
        cost_estimate=pl.CostEstimate(flops=0, bytes_accessed=0, transcendentals=0),
    )(*operands)


def local(a_blocks, b_blocks, a_extent, b_extent):
    rows, band, depth, block = a_blocks.shape
    ring = lax.axis_size("row") * lax.axis_size("col")
    rows_out = rows // lax.axis_size("rep")
    half_band = (band - 1) // 2

    def flat(x):
        return x.reshape(-1, depth, block)

    extra_size, rest_size = EXTRA_ROWS * band, REST * band + half_band
    sizes = (extra_size, rows * band - extra_size - rest_size, rest_size)
    starts = ((rows * band - extra_size, rest_size, 0), (0, extra_size, rows * band - rest_size))
    spans = list(zip(*starts))

    distance = jnp.abs(lax.broadcasted_iota(jnp.int32, b_blocks.shape, 1) - half_band)
    live = distance <= b_extent[:, None, None, None]
    b_own = b_blocks * live.astype(b_blocks.dtype)
    outer = to_outer_neighbour(b_own, ring)
    across = over_rep(b_blocks)
    peer = to_chip_peer(b_own, ring)
    turned, turned_send = turned_left(a_blocks, a_extent, rows_out)
    turned_across = over_rep(turned_send)
    across = after(across, turned_send)
    parts = (0, EARLY_PEER_ROWS * band)
    part_sizes = (EARLY_PEER_ROWS * band, (rows - EARLY_PEER_ROWS) * band)
    picks = picked(across, [*spans[:2], *zip(parts, parts)], [*sizes[:2], *part_sizes], b_extent)
    onward, across_own = picks[:2], picks[2:]
    across_outer = [to_outer_neighbour(x, ring) for x in onward]
    extra, rest = picked(after(outer, peer), [spans[0], spans[2][::-1]], [sizes[0], sizes[2]])
    extra = to_second_neighbour(extra, ring)
    across_outer.append(over_rep(rest))
    across_extra = to_second_neighbour(across_outer[0], ring)
    across_peer = [
        to_chip_peer(x if i == 0 else after(x, across_outer[0]), ring)
        for i, x in enumerate(across_own)
    ]

    def window_rows(rep_value, core_value):
        sides = ("outer", "peer") if core_value == 0 else ("peer", "outer")
        line = [(kind, i) for kind in (sides[0], "own", sides[1]) for i in range(rows)]
        extra_line = [("extra", i) for i in range(EXTRA_ROWS)]
        return extra_line + line if rep_value == 0 else line + extra_line

    def where_of(index):
        def where(rep_value, core_value):
            found = []
            for slot, (kind, i) in enumerate(window_rows(rep_value, core_value)):
                if kind not in index:
                    continue
                sources, lows, counts = index[kind]
                for source, low, count in zip(sources, lows[rep_value], counts):
                    first = max(i * band, low)
                    last = min((i + 1) * band, low + count)
                    if first < last:
                        found.append((slot, source, first - low, first - i * band, last - first))
            return sorted(found, key=lambda piece: -piece[-1])

        return where

    whole = ((0,), (0,)), (rows * band,)
    only_extra = ((0,), (0,)), (extra_size,)
    pieces = (parts, parts), part_sizes
    count = len(parts)
    total = partial_product(
        turned,
        [flat(b_own), flat(peer), flat(outer), extra],
        where_of(
            {
                "own": ((0,), *whole),
                "peer": ((1,), *whole),
                "outer": ((2,), *whole),
                "extra": ((3,), *only_extra),
            }
        ),
        None,
        rows_out,
        band,
        jnp.bfloat16,
    )
    total = partial_product(
        turned_across,
        [*across_own, *across_peer],
        where_of(
            {"own": (range(count), *pieces), "peer": (range(count, 2 * count), *pieces)}
        ),
        total,
        rows_out,
        band,
        jnp.float32,
    )
    return partial_product(
        turned_across,
        [*across_outer, across_extra],
        where_of({"outer": ((0, 1, 2), starts, sizes), "extra": ((3,), *only_extra)}),
        total,
        rows_out,
        band,
        None,
    )


def solution(mesh):
    return jax.shard_map(
        local,
        mesh=mesh,
        in_specs=(
            P(("row", "col"), None, "rep", None),
            P(("row", "col"), None, "rep", None),
            P(("row", "col")),
            P(("row", "col")),
        ),
        out_specs=P(("row", "col", "rep"), None, None, None),
        check_vma=False,
    )
```

```python
import functools

import jax
import jax.numpy as jnp
from jax import lax
from jax.experimental import pallas as pl
from jax.experimental.pallas import tpu as pltpu
from jax.sharding import PartitionSpec as P

RING = ("row", "col")
EVERY = ("row", "col", "rep")
EXTRA_ROWS = 2
EARLY_PEER_ROWS = 4
OUT_PARTS = 3
REST = 1
VMEM_LIMIT = 24 * 2**20


def to_chip_peer(x, ring):
    return lax.ppermute(x, RING, [(g, g ^ 1) for g in range(ring)])


def to_outer_neighbour(x, ring):
    return lax.ppermute(x, RING, [(g, (g + 2 * (g % 2) - 1) % ring) for g in range(ring)])


def to_second_neighbour(x, ring):
    pairs = []
    for g in range(ring):
        owner = g + 1 if g % 2 else g - 1
        pairs.append((2 * g, 2 * ((owner + 2) % ring)))
        pairs.append((2 * g + 1, 2 * ((owner - 2) % ring) + 1))
    return lax.ppermute(x, EVERY, pairs)


def over_rep(x):
    return lax.ppermute(x, "rep", [(0, 1), (1, 0)])


def turn_kernel(rows_out, extent_ref, a_ref, keep_ref, send_ref):
    rows, band, depth, block = a_ref.shape
    half_band = (band - 1) // 2
    squares = keep_ref.shape[2] // (2 * depth)
    blank = jnp.zeros((depth, block), a_ref.dtype)
    rep = lax.axis_index("rep")

    def turn(row, into_ref):
        shift = first_slot(row // rows_out, row % rows_out) % 2
        extent = extent_ref[row]

        def piece(offset):
            if not 0 <= offset < band:
                return blank
            return jnp.where(abs(offset - half_band) <= extent, a_ref[row, offset], blank)

        for square in range(squares):
            offset = 2 * square - shift
            both = jnp.concatenate([piece(offset), piece(offset + 1)], 0)
            into_ref[row % rows_out, :, square * 2 * depth : (square + 1) * 2 * depth] = both.T

    for rep_value in range(rows // rows_out):

        @pl.when(rep == rep_value)
        def _(rep_value=rep_value):
            for row in range(rows):
                turn(row, keep_ref if row // rows_out == rep_value else send_ref)


def turned_left(a_blocks, a_extent, rows_out):
    rows, band, depth, block = a_blocks.shape
    shape = jax.ShapeDtypeStruct((rows_out, block, (band + 1) * depth), a_blocks.dtype)
    return pl.pallas_call(
        functools.partial(turn_kernel, rows_out),
        out_shape=(shape, shape),
        in_specs=[
            pl.BlockSpec(memory_space=pltpu.SMEM),
            pl.BlockSpec(memory_space=pltpu.VMEM),
        ],
        out_specs=(pl.BlockSpec(memory_space=pltpu.VMEM),) * 2,
        compiler_params=pltpu.CompilerParams(vmem_limit_bytes=8 * 2**20),
        cost_estimate=pl.CostEstimate(flops=0, bytes_accessed=0, transcendentals=0),
    )(a_extent, a_blocks)


def pick_kernel(band, spans, masks, *refs):
    refs = list(refs)
    extent_ref = refs.pop(0) if masks else None
    x_ref, out_refs, sem = refs[0], refs[1:-1], refs[-1]
    half_band = (band - 1) // 2
    rep = lax.axis_index("rep")

    def copies():
        return [
            pltpu.make_async_copy(
                x_ref.at[pl.ds(jnp.where(rep == 0, low, high), out_ref.shape[0])],
                out_ref,
                sem.at[i],
            )
            for i, ((low, high), out_ref) in enumerate(zip(spans, out_refs))
        ]

    def clear_row(out_ref, at, low, high, extent):
        def clear(offset, carry):
            if low <= 0:
                out_ref[at + offset] = jnp.zeros(out_ref.shape[1:], out_ref.dtype)
            if high >= band:
                out_ref[at + band - 1 - offset] = jnp.zeros(out_ref.shape[1:], out_ref.dtype)
            return carry

        lax.fori_loop(0, half_band - extent, clear, 0)

    for copy in copies():
        copy.start()
    for copy in copies():
        copy.wait()
    if not masks:
        return
    for rep_value in range(2):

        @pl.when(rep == rep_value)
        def _(rep_value=rep_value):
            for span, out_ref in zip(spans, out_refs):
                start = span[rep_value]
                end = start + out_ref.shape[0]
                for row in range(start // band, (end + band - 1) // band):
                    at = row * band - start
                    clear_row(out_ref, at, max(-at, 0), min(end - start - at, band), extent_ref[row])


def picked(x, spans, sizes, extents=None):
    rows, band, depth, block = x.shape
    masks = extents is not None
    shapes = [jax.ShapeDtypeStruct((size, depth, block), x.dtype) for size in sizes]
    out_space = pltpu.VMEM if masks else pl.ANY
    in_specs = [pl.BlockSpec(memory_space=pltpu.SMEM)] if masks else []
    return pl.pallas_call(
        functools.partial(pick_kernel, band, spans, masks),
        out_shape=shapes,
        in_specs=in_specs + [pl.BlockSpec(memory_space=pl.ANY)],
        out_specs=[pl.BlockSpec(memory_space=out_space)] * len(sizes),
        scratch_shapes=[pltpu.SemaphoreType.DMA((len(sizes),))],
        compiler_params=pltpu.CompilerParams(vmem_limit_bytes=(4 if masks else 1) * 2**20),
        cost_estimate=pl.CostEstimate(flops=0, bytes_accessed=0, transcendentals=0),
    )(*([extents] if masks else []), x.reshape(rows * band, depth, block))


def after(x, *others):
    return lax.optimization_barrier((x, *others))[0]


def first_slot(rep_value, row):
    return row + rep_value


def product_kernel(plan, *refs):
    refs = list(refs)
    turned_ref = refs.pop(0)
    source_refs = [refs.pop(0) for _ in range(plan["sources"])]
    partial_ref = refs.pop(0) if plan["partial"] else None
    out_ref, left, window, left_sem, row_sem = refs[:5]
    final = plan["final"]
    if final:
        result, out_sem = refs[5:]
    band, rows_out = plan["band"], plan["rows_out"]
    columns, slots, depth, block = window.shape
    pairs = columns // 2
    reach = (band + 1) * depth
    width = slots * depth
    rep = lax.axis_index("rep")
    core = lax.rem(lax.axis_index("col"), 2)

    def left_copy(row, at):
        return pltpu.make_async_copy(
            turned_ref.at[row],
            left.at[pl.ds(row * block, block), pl.ds(at, reach)],
            left_sem.at[row],
        )

    def row_copy(source, at, slot, first, count, index):
        return pltpu.make_async_copy(
            source.at[pl.ds(at, count)],
            window.at[pl.ds(slot + first, count), slot],
            row_sem.at[index],
        )

    bounds = [(2 * band - 1) * i // OUT_PARTS for i in range(OUT_PARTS + 1)]

    def out_copy(part, row):
        low = bounds[part]
        count = bounds[part + 1] - low
        return pltpu.make_async_copy(
            result.at[row, pl.ds(first_slot(rep, row) + low, count)],
            out_ref.at[row, pl.ds(low, count)],
            out_sem.at[part, row],
        )

    def place_left(rep_value):
        for row in range(rows_out):
            at = first_slot(rep_value, row) // 2 * 2 * depth
            left_copy(row, at).start()
            lines = slice(row * block, (row + 1) * block)
            if at:
                left[lines, :at] = jnp.zeros((block, at), left.dtype)
            if at + reach < width:
                left[lines, at + reach :] = jnp.zeros((block, width - at - reach), left.dtype)

    def place_rows(listed):
        for index, (slot, source, at, first, count) in enumerate(listed):
            row_copy(source_refs[source], at, slot, first, count, index).start()
        blank = jnp.zeros((depth, block), window.dtype)
        taken = {slot for slot, *_ in listed}
        for pair in range(pairs):
            if 2 * pair + 1 in taken:
                window[2 * pair, 2 * pair + 1] = blank
            if 2 * pair + 1 - band in taken:
                window[2 * pair + 1, 2 * pair + 1 - band] = blank

    def multiply(ranges, some_pairs):
        for pair in some_pairs:
            total = None
            for low, high in ranges:
                first, last = max(low, 2 * pair + 1 - band), min(high, 2 * pair + 2)
                if first >= last:
                    continue
                span = (last - first) * depth
                right = jnp.concatenate(
                    [
                        window[2 * pair + side, first:last].reshape(span, block)
                        for side in range(2)
                    ],
                    1,
                )
                term = jnp.dot(
                    left[:, first * depth : last * depth],
                    right,
                    preferred_element_type=jnp.float32,
                )
                total = term if total is None else total + term
            if partial_ref is not None:
                before = partial_ref[pair].astype(jnp.float32)
                total = before if total is None else total + before
            if not final:
                out_ref[pair] = total.astype(out_ref.dtype)
                continue
            total = total.astype(result.dtype)
            for row in range(rows_out):
                for side in range(2):
                    result[row, 2 * pair + side] = total[
                        row * block : (row + 1) * block, side * block : (side + 1) * block
                    ]

    for rep_value in range(2):

        @pl.when(rep == rep_value)
        def _(rep_value=rep_value):
            place_left(rep_value)

        for core_value in range(2):

            @pl.when((rep == rep_value) & (core == core_value))
            def _(rep_value=rep_value, core_value=core_value):
                place_rows(plan["where"](rep_value, core_value))

    for row in range(rows_out):
        left_copy(row, 0).wait()
    for index, count in enumerate(plan["counts"]):
        row_copy(source_refs[0], 0, 0, 0, count, index).wait()
    parts = [range(pairs)]
    if final:
        ends = [0, *((bound - 1 + rows_out) // 2 + 1 for bound in bounds[1:-1]), pairs]
        parts = [range(low, high) for low, high in zip(ends, ends[1:])]
    for part, some_pairs in enumerate(parts):
        if len(plan["counts"]) == slots:
            multiply([(0, slots)], some_pairs)
        else:
            for rep_value in range(2):
                for core_value in range(2):

                    @pl.when((rep == rep_value) & (core == core_value))
                    def _(rep_value=rep_value, core_value=core_value, some_pairs=some_pairs):
                        taken = sorted({slot for slot, *_ in plan["where"](rep_value, core_value)})
                        lows = [slot for slot in taken if slot - 1 not in taken]
                        highs = [slot + 1 for slot in taken if slot + 1 not in taken]
                        multiply(list(zip(lows, highs)), some_pairs)

        if final:
            for row in range(rows_out):
                out_copy(part, row).start()
    if final:
        for part in range(OUT_PARTS):
            for row in range(rows_out):
                out_copy(part, row).wait()


def partial_product(turned, sources, where, partial, rows_out, band, kind):
    depth, block = sources[0].shape[1:]
    slots = rows_out + band
    columns = slots + band - 1
    counts = [count for *_, count in where(0, 0)]
    final = kind is None
    plan = {
        "sources": len(sources),
        "where": where,
        "counts": counts,
        "band": band,
        "rows_out": rows_out,
        "partial": partial is not None,
        "final": final,
    }
    operands = [turned, *sources]
    in_specs = [pl.BlockSpec(memory_space=pl.ANY)] * len(operands)
    if partial is not None:
        operands.append(partial)
        in_specs.append(pl.BlockSpec(memory_space=pltpu.VMEM))
    scratch = [
        pltpu.VMEM((rows_out * block, slots * depth), jnp.bfloat16),
        pltpu.VMEM((columns, slots, depth, block), jnp.bfloat16),
        pltpu.SemaphoreType.DMA((rows_out,)),
        pltpu.SemaphoreType.DMA((len(counts),)),
    ]
    if final:
        out_shape = jax.ShapeDtypeStruct((rows_out, 2 * band - 1, block, block), jnp.bfloat16)
        out_spec = pl.BlockSpec(memory_space=pl.ANY)
        scratch += [
            pltpu.VMEM((rows_out, columns, block, block), jnp.bfloat16),
            pltpu.SemaphoreType.DMA((OUT_PARTS, rows_out)),
        ]
    else:
        out_shape = pltpu.VMEM((columns // 2, rows_out * block, 2 * block), kind)
        out_spec = pl.BlockSpec(memory_space=pltpu.VMEM)
    return pl.pallas_call(
        functools.partial(product_kernel, plan),
        out_shape=out_shape,
        in_specs=in_specs,
        out_specs=out_spec,
        scratch_shapes=scratch,
        compiler_params=pltpu.CompilerParams(vmem_limit_bytes=VMEM_LIMIT),
        cost_estimate=pl.CostEstimate(flops=0, bytes_accessed=0, transcendentals=0),
    )(*operands)


def local(a_blocks, b_blocks, a_extent, b_extent):
    rows, band, depth, block = a_blocks.shape
    ring = lax.axis_size("row") * lax.axis_size("col")
    rows_out = rows // lax.axis_size("rep")
    half_band = (band - 1) // 2

    def flat(x):
        return x.reshape(-1, depth, block)

    extra_size, rest_size = EXTRA_ROWS * band, REST * band + half_band
    sizes = (extra_size, rows * band - extra_size - rest_size, rest_size)
    starts = ((rows * band - extra_size, rest_size, 0), (0, extra_size, rows * band - rest_size))
    spans = list(zip(*starts))

    distance = jnp.abs(lax.broadcasted_iota(jnp.int32, b_blocks.shape, 1) - half_band)
    live = distance <= b_extent[:, None, None, None]
    b_own = b_blocks * live.astype(b_blocks.dtype)
    outer = to_outer_neighbour(b_own, ring)
    across = over_rep(b_blocks)
    peer = to_chip_peer(b_own, ring)
    turned, turned_send = turned_left(a_blocks, a_extent, rows_out)
    turned_across = over_rep(turned_send)
    across = after(across, turned_send)
    parts = (0, EARLY_PEER_ROWS * band)
    part_sizes = (EARLY_PEER_ROWS * band, (rows - EARLY_PEER_ROWS) * band)
    picks = picked(across, [*spans[:2], *zip(parts, parts)], [*sizes[:2], *part_sizes], b_extent)
    onward, across_own = picks[:2], picks[2:]
    across_outer = [to_outer_neighbour(x, ring) for x in onward]
    extra, rest = picked(after(outer, peer), [spans[0], spans[2][::-1]], [sizes[0], sizes[2]])
    extra = to_second_neighbour(extra, ring)
    across_outer.append(over_rep(rest))
    across_extra = to_second_neighbour(across_outer[0], ring)
    across_peer = [
        to_chip_peer(x if i == 0 else after(x, across_outer[0]), ring)
        for i, x in enumerate(across_own)
    ]

    def window_rows(rep_value, core_value):
        sides = ("outer", "peer") if core_value == 0 else ("peer", "outer")
        line = [(kind, i) for kind in (sides[0], "own", sides[1]) for i in range(rows)]
        extra_line = [("extra", i) for i in range(EXTRA_ROWS)]
        return extra_line + line if rep_value == 0 else line + extra_line

    def where_of(index):
        def where(rep_value, core_value):
            found = []
            for slot, (kind, i) in enumerate(window_rows(rep_value, core_value)):
                if kind not in index:
                    continue
                sources, lows, counts = index[kind]
                for source, low, count in zip(sources, lows[rep_value], counts):
                    first = max(i * band, low)
                    last = min((i + 1) * band, low + count)
                    if first < last:
                        found.append((slot, source, first - low, first - i * band, last - first))
            return sorted(found, key=lambda piece: -piece[-1])

        return where

    whole = ((0,), (0,)), (rows * band,)
    only_extra = ((0,), (0,)), (extra_size,)
    pieces = (parts, parts), part_sizes
    count = len(parts)
    total = partial_product(
        turned,
        [flat(b_own), flat(peer), flat(outer), extra],
        where_of(
            {
                "own": ((0,), *whole),
                "peer": ((1,), *whole),
                "outer": ((2,), *whole),
                "extra": ((3,), *only_extra),
            }
        ),
        None,
        rows_out,
        band,
        jnp.bfloat16,
    )
    total = partial_product(
        turned_across,
        [*across_own, *across_peer, across_outer[0]],
        where_of(
            {
                "own": (range(count), *pieces),
                "peer": (range(count, 2 * count), *pieces),
                "outer": ((2 * count,), [x[:1] for x in starts], sizes[:1]),
            }
        ),
        total,
        rows_out,
        band,
        jnp.float32,
    )
    return partial_product(
        turned_across,
        [*across_outer[1:], across_extra],
        where_of(
            {
                "outer": ((0, 1), [x[1:] for x in starts], sizes[1:]),
                "extra": ((2,), *only_extra),
            }
        ),
        total,
        rows_out,
        band,
        None,
    )


def solution(mesh):
    return jax.shard_map(
        local,
        mesh=mesh,
        in_specs=(
            P(("row", "col"), None, "rep", None),
            P(("row", "col"), None, "rep", None),
            P(("row", "col")),
            P(("row", "col")),
        ),
        out_specs=P(("row", "col", "rep"), None, None, None),
        check_vma=False,
    )
```
